256 devices in a mesh: obs: 32 (over x, y, core), row: 8 (over z).
Axes of the slice: x: 4, y: 4, z: 8, core: 2. Of those that a mesh axis runs over, the one named last changes fastest.
Arguments:
- camera_jacobian: float32 [18, 262144], P(None, ('obs', 'row')), may hold values from -0.75 to 0.75
- point_jacobian: float32 [6, 262144], P(None, ('obs', 'row')), may hold values from -6 to 6
- residual: float32 [2, 262144], P(None, ('obs', 'row')), may hold values from -6 to 6
- send_order: int32 [262144], P(('obs', 'row')), may hold values from 0 to 1023, as said below
- camera_of: int32 [262144], P(('obs', 'row')), may hold values from 0 to 127, as said below
- track_of: int32 [262144], P(('obs', 'row')), may hold values from 0 to 511, as said below
- partner: int32 [7, 262144], P(None, ('obs', 'row')), may hold values from 0 to 1023, as said below
- pair_slot: int32 [7, 262144], P(None, ('obs', 'row')), may hold values from 0 to 1792, as said below
Outputs:
- camera_hessian: float32 [81, 4096], P(None, ('obs', 'row'))
- camera_gradient: float32 [9, 4096], P(None, ('obs', 'row'))
- pair_hessian: float32 [81, 57344], P(None, ('obs', 'row'))
The draws below stay inside these ranges and needn't reach their ends.
Inputs may be any that keep to these rules, and one draw needn't show every extreme that they name: `send_order`: on each device a permutation of the device's 1024 observations. `camera_of`: A device's observations are ordered by camera. `track_of`: local track of each received slot of one track owner; a track has 2 to 8 observations, at most one from each source obs index, from cyclically consecutive source obs indices; some track ids are unused. partner[k] of a received slot is the slot of the k-th other observation of its track in track order, or the slot itself where the track has fewer than k + 2 observations. pair_slot[k] of a send slot is c * 14 + o, where c is the observation's camera and o encodes its partner's camera; 1792 exactly where partner[k] is the slot itself.
All inputs are finite; a program needn't handle non-finite values.
Results may differ from the reference program's by a relative error of at most 0.00014.
Values sent between devices are 32-bit elements; how exact they have to be, the bound alone decides.
No kernel may reach another device: no remote copies, remote signals or barrier semaphores. Data moves between devices by JAX's collectives and lax.ppermute only.
A program may use at most 64 MiB of HBM per device.

```python
import jax
import jax.numpy as jnp

OBS_DEV = 1024
CAM_ROW = 16
CAMP = 9
PNTP = 3
LMAX = 8
NBR = 14
NOBS = 262144
N_OBS = 32
N_ROW = 8


slot_track = [[0, 0, 0, 0, 0, 0, 0, 0], [0, 0, 0, 0, 1, 1, 1, 1], [0, 0, 0, 0, 0, 1, 1, 1], [0, 0, 0, 0, 0, 0, 1, 1], [0, 0, 1, 1, 2, 2, 3, 3], [0, 0, 0, 1, 1, 1, 2, 2], [0, 0, 0, 0, 1, 1, 2, 2]]


slot_place = [[0, 1, 2, 3, 4, 5, 6, 7], [0, 1, 2, 3, 0, 1, 2, 3], [0, 1, 2, 3, 4, 0, 1, 2], [0, 1, 2, 3, 4, 5, 0, 1], [0, 1, 0, 1, 0, 1, 0, 1], [0, 1, 2, 0, 1, 2, 0, 1], [0, 1, 2, 3, 0, 1, 0, 1]]


slot_length = [[8, 8, 8, 8, 8, 8, 8, 8], [4, 4, 4, 4, 4, 4, 4, 4], [5, 5, 5, 5, 5, 3, 3, 3], [6, 6, 6, 6, 6, 6, 2, 2], [2, 2, 2, 2, 2, 2, 2, 2], [3, 3, 3, 3, 3, 3, 2, 2], [4, 4, 4, 4, 2, 2, 2, 2]]


def layout(key):
    base_key = jax.random.fold_in(key, 11)
    subkeys = jax.random.split(base_key, 5)
    per_peer = OBS_DEV // N_OBS
    block_count = N_OBS // 8
    camera_count = CAM_ROW * N_ROW
    slot_count = camera_count * NBR
    rotation = jax.random.randint(subkeys[0], (N_ROW, N_OBS, per_peer, 1), 0, 8)
    pattern = jax.random.randint(subkeys[1], (N_ROW, N_OBS, per_peer, block_count), 0, 7)
    dense_row = jax.random.randint(subkeys[2], (), 0, N_ROW)
    row_ids = jnp.arange(N_ROW, dtype=jnp.int32).reshape(N_ROW, 1, 1, 1)
    pattern = jnp.where(row_ids == dense_row, 0, pattern)
    start_camera = jax.random.randint(subkeys[3], (N_ROW, N_OBS, per_peer, block_count * 4), 0, camera_count - 1)
    scores = jax.random.randint(subkeys[4], (N_ROW, N_OBS, N_OBS, per_peer), 0, 1 << 20) * per_peer
    scores = scores + jnp.arange(per_peer, dtype=jnp.int32)
    place = jnp.argsort(scores, axis=3).astype(jnp.int32)
    inverse = jnp.argsort(place, axis=3).astype(jnp.int32)
    sources = jnp.arange(N_OBS, dtype=jnp.int32).reshape(1, 1, 1, N_OBS)
    column = (sources - rotation) % N_OBS
    block = column // 8
    within = column % 8
    kind = jnp.take_along_axis(pattern, block, axis=3)
    track_sub = jnp.asarray(slot_track, dtype=jnp.int32)[kind, within]
    position = jnp.asarray(slot_place, dtype=jnp.int32)[kind, within]
    length = jnp.asarray(slot_length, dtype=jnp.int32)[kind, within]
    track_id = jnp.arange(per_peer, dtype=jnp.int32).reshape(1, 1, per_peer, 1) * (block_count * 4) + block * 4 + track_sub
    start_local = jnp.take_along_axis(start_camera, block * 4 + track_sub, axis=3)
    first_source = (sources - position) % N_OBS
    capture = first_source + N_OBS * start_local + position
    camera_local = capture // N_OBS
    place_by_source = jnp.transpose(place, (0, 1, 3, 2))
    self_slot = sources * per_peer + place_by_source
    partner_slots = []
    pair_slots = []
    for partner_rank in range(7):
        other = partner_rank + (partner_rank >= position).astype(jnp.int32)
        valid = other < length
        other_source = (sources + other - position) % N_OBS
        other_slot = other_source * per_peer + jnp.take_along_axis(place_by_source, other_source, axis=3)
        partner_slots.append(jnp.where(valid, other_slot, self_slot))
        offset = other - position
        neighbour = jnp.where(offset < 0, offset + 7, offset + 6)
        pair_slots.append(jnp.where(valid, camera_local * NBR + neighbour, slot_count))

    def to_owner(values):
        return jnp.take_along_axis(jnp.transpose(values, (0, 1, 3, 2)), inverse, axis=3)

    def owner_flat(values):
        return jnp.transpose(to_owner(values), (1, 0, 2, 3)).reshape(-1)

    def image_flat(values):
        return jnp.transpose(to_owner(values), (2, 0, 1, 3)).reshape(-1)
    track_of = owner_flat(track_id).astype(jnp.int32)
    partner = jnp.stack([owner_flat(entry) for entry in partner_slots]).astype(jnp.int32)
    pair_slot = jnp.stack([image_flat(entry) for entry in pair_slots]).astype(jnp.int32)
    camera_send = image_flat(camera_local).reshape(N_OBS * N_ROW, OBS_DEV)
    order_keys = camera_send * OBS_DEV + jnp.arange(OBS_DEV, dtype=jnp.int32)
    sorted_pos = jnp.argsort(order_keys, axis=1).astype(jnp.int32)
    camera_of = jnp.take_along_axis(camera_send, sorted_pos, axis=1).astype(jnp.int32)
    send_order = jnp.argsort(sorted_pos, axis=1).astype(jnp.int32)
    return (send_order.reshape(-1), camera_of.reshape(-1), track_of, partner, pair_slot)


def draw_send_order(key, part):
    return layout(key)[0]


def draw_camera_of(key, part):
    return layout(key)[1]


def draw_track_of(key, part):
    return layout(key)[2]


def draw_partner(key, part):
    return layout(key)[3]


def draw_pair_slot(key, part):
    return layout(key)[4]


def block_scale(own_key, shape, cuts, least, largest):
    gain, own = 1.0, jax.random.fold_in(own_key, 6)
    for dim, blocks in cuts:
        draws = jnp.exp(jax.random.uniform(jax.random.fold_in(own, dim), (blocks,), jnp.float32, least / len(cuts), largest / len(cuts)))
        gain = gain * jnp.repeat(draws, shape[dim] // blocks).reshape([-1 if axis == dim else 1 for axis in range(len(shape))])
    return gain


def bell_draw(stream_key, shape, deviation, most, cuts=(), held_as=jnp.bfloat16):
    result = deviation * jax.random.normal(stream_key, shape, jnp.float32)
    if cuts:
        result = result * block_scale(stream_key, shape, cuts, -0.22, 0.18)
    return jnp.clip(result, -most, most).astype(held_as)


def setup_inputs(seed: int = 0) -> dict:
    arg_keys = jax.random.split(jax.random.key(seed), 9)
    return {
        "camera_jacobian": bell_draw(arg_keys[0], (2 * CAMP, NOBS), 0.125, 0.75, ((1, 256),), jnp.float32),
        "point_jacobian": bell_draw(arg_keys[1], (2 * PNTP, NOBS), 1.0, 6.0, ((1, 256),), jnp.float32),
        "residual": bell_draw(arg_keys[2], (2, NOBS), 1.0, 6.0, ((1, 256),), jnp.float32),
        "send_order": draw_send_order(jax.random.fold_in(arg_keys[8], 71), 0),
        "camera_of": draw_camera_of(jax.random.fold_in(arg_keys[8], 71), 0),
        "track_of": draw_track_of(jax.random.fold_in(arg_keys[8], 71), 0),
        "partner": draw_partner(jax.random.fold_in(arg_keys[8], 71), 0),
        "pair_slot": draw_pair_slot(jax.random.fold_in(arg_keys[8], 71), 0),
    }


damping = 1.0

def eliminate(camera_rows, point_rows, resid_rows, track_of, track_count):
    camera = camera_rows.reshape(2, 9, -1)
    point_jac = point_rows.reshape(2, 3, -1)
    normal = jnp.stack([point_jac[0, 0] * point_jac[0, 0] + point_jac[1, 0] * point_jac[1, 0], point_jac[0, 0] * point_jac[0, 1] + point_jac[1, 0] * point_jac[1, 1], point_jac[0, 0] * point_jac[0, 2] + point_jac[1, 0] * point_jac[1, 2], point_jac[0, 1] * point_jac[0, 1] + point_jac[1, 1] * point_jac[1, 1], point_jac[0, 1] * point_jac[0, 2] + point_jac[1, 1] * point_jac[1, 2], point_jac[0, 2] * point_jac[0, 2] + point_jac[1, 2] * point_jac[1, 2], point_jac[0, 0] * resid_rows[0] + point_jac[1, 0] * resid_rows[1], point_jac[0, 1] * resid_rows[0] + point_jac[1, 1] * resid_rows[1], point_jac[0, 2] * resid_rows[0] + point_jac[1, 2] * resid_rows[1]])
    totals = jnp.zeros((9, track_count), jnp.float32).at[:, track_of].add(normal)
    pivot_first = jnp.sqrt(totals[0] + damping)
    lower_one = totals[1] / pivot_first
    lower_two = totals[2] / pivot_first
    pivot_second = jnp.sqrt(totals[3] + damping - lower_one * lower_one)
    lower_mid = (totals[4] - lower_two * lower_one) / pivot_second
    pivot_third = jnp.sqrt(totals[5] + damping - lower_two * lower_two - lower_mid * lower_mid)
    solved_one = totals[6] / pivot_first
    solved_two = (totals[7] - lower_one * solved_one) / pivot_second
    solved_three = (totals[8] - lower_two * solved_one - lower_mid * solved_two) / pivot_third
    per_track = jnp.stack([pivot_first, lower_one, lower_two, pivot_second, lower_mid, pivot_third, solved_one, solved_two, solved_three])
    per_obs = per_track[:, track_of]
    weights = camera[0][:, None, :] * point_jac[0][None, :, :] + camera[1][:, None, :] * point_jac[1][None, :, :]
    column_one = weights[:, 0] / per_obs[0]
    column_two = (weights[:, 1] - per_obs[1] * column_one) / per_obs[3]
    column_three = (weights[:, 2] - per_obs[2] * column_one - per_obs[4] * column_two) / per_obs[5]
    factor = jnp.stack([column_one, column_two, column_three])
    point_shift = column_one * per_obs[6] + column_two * per_obs[7] + column_three * per_obs[8]
    return (factor, point_shift)

def camera_terms(camera_rows, resid_rows, factor, point_shift):
    camera = camera_rows.reshape(2, 9, -1)
    normal = camera[0][:, None, :] * camera[0][None, :, :] + camera[1][:, None, :] * camera[1][None, :, :]
    schur_part = factor[0][:, None, :] * factor[0][None, :, :] + factor[1][:, None, :] * factor[1][None, :, :] + factor[2][:, None, :] * factor[2][None, :, :]
    gradient = camera[0] * resid_rows[0] + camera[1] * resid_rows[1] - point_shift
    return jnp.concatenate([(normal - schur_part).reshape(81, -1), gradient], axis=0)

def pair_product(left, right):
    total = left[0][:, None, :] * right[0][None, :, :] + left[1][:, None, :] * right[1][None, :, :] + left[2][:, None, :] * right[2][None, :, :]
    return -total.reshape(81, -1)

def reference(camera_jacobian, point_jacobian, residual, send_order, camera_of, track_of, partner, pair_slot):
    device_count = N_OBS * N_ROW
    per_peer = OBS_DEV // N_OBS
    camera_count = CAM_ROW * N_ROW
    slot_count = camera_count * NBR
    send_perm = send_order.reshape(device_count, OBS_DEV)

    def outgoing(values):
        shaped = values.reshape(values.shape[0], device_count, OBS_DEV)
        return jnp.take_along_axis(shaped, jnp.broadcast_to(send_perm[None], shaped.shape), axis=2)

    def regroup(values):
        height = values.shape[0]
        moved = values.reshape(height, N_OBS, N_ROW, N_OBS, per_peer).transpose(0, 3, 2, 1, 4)
        return moved.reshape(height, device_count, OBS_DEV)
    camera_sent = outgoing(camera_jacobian)
    point_sent = outgoing(point_jacobian)
    resid_sent = outgoing(residual)
    tracks = track_of.reshape(device_count, OBS_DEV)
    factor, point_shift = jax.vmap(eliminate, in_axes=(1, 1, 1, 0, None), out_axes=(2, 1))(regroup(camera_sent), regroup(point_sent), regroup(resid_sent), tracks, OBS_DEV // 2)
    factor_back = regroup(factor.reshape(27, -1)).reshape(3, 9, -1)
    shift_back = regroup(point_shift.reshape(9, -1)).reshape(9, -1)
    local_terms = camera_terms(camera_sent.reshape(18, -1), resid_sent.reshape(2, -1), factor_back, shift_back)
    camera_ids = jnp.take_along_axis(camera_of.reshape(device_count, OBS_DEV), send_perm, axis=1)
    group_of = (jnp.arange(device_count) // N_ROW).astype(jnp.int32)
    camera_index = (group_of[:, None] * camera_count + camera_ids).astype(jnp.int32).reshape(-1)
    camera_sum = jnp.zeros((90, N_OBS * camera_count), jnp.float32).at[:, camera_index].add(local_terms)
    flat_factor = factor.reshape(3, 9, device_count, OBS_DEV)
    partners = partner.reshape(LMAX - 1, device_count, OBS_DEV)
    slot_index = pair_slot.reshape(LMAX - 1, device_count, OBS_DEV)
    group_base = (group_of * slot_count).astype(jnp.int32)[:, None]
    pair_total = jnp.zeros((81, N_OBS * slot_count + 1), jnp.float32)
    for partner_rank in range(LMAX - 1):
        chosen = jnp.take_along_axis(flat_factor, jnp.broadcast_to(partners[partner_rank][None, None], flat_factor.shape), axis=3)
        block_values = pair_product(flat_factor.reshape(3, 9, -1), chosen.reshape(3, 9, -1))
        arrived = regroup(block_values).reshape(81, -1)
        target = jnp.where(slot_index[partner_rank] == slot_count, N_OBS * slot_count, group_base + slot_index[partner_rank]).astype(jnp.int32).reshape(-1)
        pair_total = pair_total.at[:, target].add(arrived)
    return (camera_sum[:81], camera_sum[81:], pair_total[:, :N_OBS * slot_count])
```

```python
import jax
import jax.numpy as jnp
from jax import lax
from jax.experimental import pallas as pl
from jax.experimental.pallas import tpu as pltpu
from jax.sharding import PartitionSpec as P

CAM_ROW = 16
NBR = 14
RANKS = 7
LANES = 128
GROUP = 32
SLOTS = 1024
CHUNKS = SLOTS // LANES
ROWS_IN = 8
ROWS_BACK = 40
USED_BACK = 33
SIDE = 144
BLOCK = 176
damping = 1.0
F32 = jnp.float32
BF16 = jnp.bfloat16


def lane_groups():
    return lax.broadcasted_iota(jnp.int32, (8, LANES), 1) // GROUP


def regroup(parts, group, sign):
    outs = []
    for a in range(4):
        out = parts[a]
        for b in range(4):
            if b != a:
                out = jnp.where(group == b, pltpu.roll(parts[b], ((b - a) * GROUP) % LANES, 1), out)
        outs.append(out)
    return outs


def pack_kernel(jc, jp, err, cam, order, msg, own, rows):
    rows[0:18, :] = jc[...]
    rows[18:24, :] = jp[...]
    rows[24:26, :] = err[...]
    rows[26:27, :] = cam[...].astype(F32)
    rows[27:32, :] = jnp.zeros((5, SLOTS), F32)
    group = lane_groups()

    def chunk(d, _):
        at = pl.multiple_of(d * LANES, LANES)
        idx = jnp.broadcast_to(order[0:1, pl.ds(at, LANES)], (8, LANES))
        part = idx // LANES
        lane = idx % LANES
        tiles = []
        for t in range(4):
            acc = jnp.zeros((8, LANES), F32)
            for s in range(CHUNKS):
                got = jnp.take_along_axis(rows[t * 8 : t * 8 + 8, s * LANES : (s + 1) * LANES], lane, axis=1)
                acc = jnp.where(part == s, got, acc)
            own[t * 8 : t * 8 + 8, pl.ds(at, LANES)] = acc
            tiles.append(acc)
        for m, tile in enumerate(regroup(tiles, group, 1)):
            msg[pl.ds(pl.multiple_of((d * 4 + m) * ROWS_IN, 8), 8), :] = tile
        return 0

    lax.fori_loop(0, CHUNKS, chunk, 0)


ROLLS = (0, 1, 2, 6, 7)


def owner_kernel(owned, partner, msg, slots, turned, near, back):
    group = lane_groups()
    for r in range(8):
        slots[pl.ds(r, RANKS, stride=8), :] = partner[:, r * LANES : (r + 1) * LANES]
    for row in range(ROWS_IN):
        ins = [owned[pl.ds(m * ROWS_IN + row, 8, stride=4 * ROWS_IN), :] for m in range(4)]
        for t, tile in enumerate(regroup(ins, group, 1)):
            u = t * 8 + row
            if u < 26:
                for n, d in enumerate(ROLLS):
                    turned[n * 26 + u] = tile if d == 0 else pltpu.roll(tile, 8 - d, 0)
    here = lax.broadcasted_iota(jnp.int32, (8, LANES), 0)
    self_slot = here * LANES + lax.broadcasted_iota(jnp.int32, (8, LANES), 1)

    def picks(k):
        idx = slots[pl.ds(pl.multiple_of(k * 8, 8), 8), :]
        step = (idx // LANES - here) % 8
        return idx != self_slot, idx % LANES, [step == d for d in ROLLS]

    def pick(u, lane, masks):
        out = jnp.take_along_axis(turned[u], lane, axis=1)
        for n in range(1, len(ROLLS)):
            out = jnp.where(masks[n], jnp.take_along_axis(turned[n * 26 + u], lane, axis=1), out)
        return out

    def normal(p, e):
        out = []
        for a in range(3):
            for b in range(a, 3):
                out.append(p[a] * p[b] + p[3 + a] * p[3 + b])
        for a in range(3):
            out.append(p[a] * e[0] + p[3 + a] * e[1])
        return out

    mine = [turned[18 + n] for n in range(8)]

    def first(k, total):
        valid, lane, masks = picks(k)
        got = [jnp.where(valid, pick(18 + n, lane, masks), 0.0) for n in range(8)]
        for n in range(6):
            near[k * 6 + n] = got[n]
        return tuple(x + y for x, y in zip(total, normal(got[:6], got[6:])))

    v00, v01, v02, v11, v12, v22, b0, b1, b2 = lax.fori_loop(0, RANKS, first, tuple(normal(mine[:6], mine[6:])))
    i0 = 1.0 / jnp.sqrt(v00 + damping)
    l10 = v01 * i0
    l20 = v02 * i0
    i1 = 1.0 / jnp.sqrt(v11 + damping - l10 * l10)
    l21 = (v12 - l20 * l10) * i1
    i2 = 1.0 / jnp.sqrt(v22 + damping - l20 * l20 - l21 * l21)

    def forward(x0, x1, x2):
        y0 = x0 * i0
        y1 = (x1 - l10 * y0) * i1
        y2 = (x2 - l20 * y0 - l21 * y1) * i2
        return y0, y1, y2

    def inner(x, y):
        return x[0] * y[0] + x[1] * y[1] + x[2] * y[2]

    h = forward(b0, b1, b2)
    g = [forward(*mine[0:3]), forward(*mine[3:6])]
    back[126] = inner(g[0], g[0])
    back[127] = inner(g[0], g[1])
    back[128] = inner(g[1], g[1])
    back[129] = inner(g[0], h)
    back[130] = inner(g[1], h)
    back[131] = jnp.zeros((8, LANES), F32)

    def second(k, _):
        valid, lane, masks = picks(k)
        p = [near[k * 6 + n] for n in range(6)]
        o = [forward(*p[0:3]), forward(*p[3:6])]
        mix = [[-inner(g[a], o[b]) for b in range(2)] for a in range(2)]
        for q in range(9):
            c0 = pick(q, lane, masks)
            c1 = pick(9 + q, lane, masks)
            for a in range(2):
                back[k * 18 + a * 9 + q] = mix[a][0] * c0 + mix[a][1] * c1
        return 0

    lax.fori_loop(0, RANKS, second, 0)

    def emit(row, _):
        tiles = [back[row * 4 + t] for t in range(4)]
        for m, tile in enumerate(regroup(tiles, group, 1)):
            msg[pl.ds(m * ROWS_BACK + row, 8, stride=4 * ROWS_BACK), :] = tile
        return 0

    lax.fori_loop(0, USED_BACK, emit, 0)


def build_right(back, own, pair_slot, right_hi, right_lo, flat):
    group = lane_groups()
    low = lax.broadcasted_iota(jnp.int32, (8, LANES), 0)
    offsets = [low, low + 8]

    def chunk(d, _):
        at = pl.multiple_of(d * LANES, LANES)
        for b in range(ROWS_BACK // 8):
            ins = [back[pl.ds(pl.multiple_of((d * 4 + m) * ROWS_BACK + b * 8, 8), 8), :] for m in range(4)]
            for t, tile in enumerate(regroup(ins, group, 1)):
                flat[t * ROWS_BACK + b * 8 : t * ROWS_BACK + b * 8 + 8, :] = tile

        def spread(u):
            row = (u % 4) * ROWS_BACK + u // 4
            return jnp.broadcast_to(flat[row : row + 1, :], (8, LANES))

        def mine(u):
            return jnp.broadcast_to(own[u : u + 1, pl.ds(at, LANES)], (8, LANES))

        cam = mine(26).astype(jnp.int32)
        hits = []
        for k in range(RANKS):
            slot = jnp.broadcast_to(pair_slot[k : k + 1, pl.ds(at, LANES)], (8, LANES))
            o = jnp.where(slot == CAM_ROW * 8 * NBR, -1, slot - cam * NBR)
            hits.append([o == off for off in offsets])
        m00, m01, m11 = spread(126), spread(127), spread(128)
        grad = [mine(24) - spread(129), mine(25) - spread(130)]
        for q in range(9):
            c0, c1 = mine(q), mine(9 + q)
            diag = [c0 - m00 * c0 - m01 * c1, c1 - m01 * c0 - m11 * c1]
            for i in range(2):
                halves = [jnp.zeros((8, LANES), F32), jnp.where(low == 6, diag[i], 0.0)]
                if q == 0:
                    halves[1] = jnp.where(low == 7, grad[i], halves[1])
                for k in range(RANKS):
                    n = spread(k * 18 + i * 9 + q)
                    halves = [x + jnp.where(hit, n, 0.0) for x, hit in zip(halves, hits[k])]
                value = jnp.concatenate(halves, axis=0)
                hi = value.astype(BF16)
                at2 = pl.multiple_of(d * 2 * LANES + i * LANES, LANES)
                right_hi[q * 16 : q * 16 + 16, pl.ds(at2, LANES)] = hi
                right_lo[q * 16 : q * 16 + 16, pl.ds(at2, LANES)] = (value - hi.astype(F32)).astype(BF16)
        return 0

    lax.fori_loop(0, CHUNKS, chunk, 0)


def dot_t(x, y):
    return lax.dot_general(x, y, (((1,), (1,)), ((), ())), preferred_element_type=F32)


def build_block(dest, own, right_hi, right_lo, left_hi, left_lo, wide, out, base):
    low = lax.broadcasted_iota(jnp.int32, (16, LANES), 0).astype(F32) + (dest * CAM_ROW).astype(F32)

    def chunk(d, _):
        at = pl.multiple_of(d * LANES, LANES)
        hit = jnp.broadcast_to(own[26:27, pl.ds(at, LANES)], (16, LANES)) == low
        for i in range(2):
            at2 = pl.multiple_of(d * 2 * LANES + i * LANES, LANES)
            for p in range(9):
                u = i * 9 + p
                value = jnp.broadcast_to(own[u : u + 1, pl.ds(at, LANES)], (16, LANES))
                value = jnp.where(hit, value, 0.0)
                hi = value.astype(BF16)
                left_hi[p * 16 : p * 16 + 16, pl.ds(at2, LANES)] = hi
                left_lo[p * 16 : p * 16 + 16, pl.ds(at2, LANES)] = (value - hi.astype(F32)).astype(BF16)
        return 0

    lax.fori_loop(0, CHUNKS, chunk, 0)
    total = dot_t(left_hi[...], right_hi[...]) + (
        dot_t(left_hi[...], right_lo[...]) + dot_t(left_lo[...], right_hi[...])
    )
    out[base : base + SIDE, :] = total[:, :LANES]
    wide[:, 0:16] = total[:, LANES:]
    lane = lax.broadcasted_iota(jnp.int32, (16, LANES), 1)
    tail = wide[0:16, :]
    for p in range(1, 8):
        tail = jnp.where(lane // 16 == p, pltpu.roll(wide[p * 16 : p * 16 + 16, :], p * 16, 1), tail)
    out[base + SIDE : base + SIDE + 16, :] = tail
    out[base + SIDE + 16 : base + BLOCK, :] = wide[128:144, :]


def camera_kernel(back, own, pair_slot, out, right_hi, right_lo, left_hi, left_lo, wide, flat):
    build_right(back, own, pair_slot, right_hi, right_lo, flat)
    wide[...] = jnp.zeros((SIDE, LANES), F32)
    for dest in range(8):
        build_block(jnp.int32(dest), own, right_hi, right_lo, left_hi, left_lo, wide, out, dest * BLOCK)


def final_kernel(parts, hess, grad, pair, body, last, rows):
    total = parts[0:BLOCK, :]
    for n in range(1, 8):
        total = total + parts[n * BLOCK : (n + 1) * BLOCK, :]
    body[...] = total
    for p in range(8):
        piece = body[SIDE : SIDE + 16, :]
        last[p * 16 : p * 16 + 16, :] = piece if p == 0 else pltpu.roll(piece, (LANES - p * 16) % LANES, 1)
    last[128:144, :] = body[SIDE + 16 : BLOCK, :]
    lane = lax.broadcasted_iota(jnp.int32, (9, LANES), 1)
    grads = jnp.zeros((9, LANES), F32)
    for q in range(9):
        halves = [jnp.zeros((9, LANES), F32), jnp.zeros((9, LANES), F32)]
        diag = jnp.zeros((9, LANES), F32)
        for c in range(CAM_ROW):
            ref, at = (body, q * 16) if q < 8 else (last, 0)
            x = ref[pl.ds(c, 9, stride=16), :]
            turn = pltpu.roll(x, (c * NBR - at) % LANES, 1)
            for half in range(2):
                lo, hi = c * NBR - half * LANES, (c + 1) * NBR - half * LANES
                if hi > 0 and lo < LANES:
                    halves[half] = jnp.where((lane >= lo) & (lane < hi), turn, halves[half])
            diag = jnp.where(lane == c, pltpu.roll(x, (c - at - 14) % LANES, 1), diag)
            if q == 0:
                grads = jnp.where(lane == c, pltpu.roll(x, (c - at - 15) % LANES, 1), grads)
        for n, x in enumerate((halves[0], halves[1], diag)):
            rows[pl.ds(n * 88 + q, 9, stride=9), :] = x
    pair[:, 0:LANES] = rows[0:81, :]
    pair[:, LANES : CAM_ROW * NBR] = rows[88:169, : CAM_ROW * NBR - LANES]
    hess[...] = rows[176:257, :CAM_ROW]
    grad[...] = grads[:, :CAM_ROW]


def on_device(
    camera_jacobian, point_jacobian, residual, send_order, camera_of, track_of, partner, pair_slot
):
    peers = lax.axis_size("obs")
    msg, own = pl.pallas_call(
        pack_kernel,
        out_shape=(
            jax.ShapeDtypeStruct((peers * ROWS_IN, LANES), F32),
            jax.ShapeDtypeStruct((32, SLOTS), F32),
        ),
        scratch_shapes=[pltpu.VMEM((32, SLOTS), F32)],
        name="pack",
    )(camera_jacobian, point_jacobian, residual, camera_of.reshape(1, SLOTS), send_order.reshape(1, SLOTS))
    owned = lax.all_to_all(msg.reshape(peers, ROWS_IN, LANES), "obs", 0, 0, tiled=True)
    returned = pl.pallas_call(
        owner_kernel,
        out_shape=jax.ShapeDtypeStruct((peers * ROWS_BACK, LANES), F32),
        scratch_shapes=[
            pltpu.VMEM((RANKS * 8, LANES), jnp.int32),
            pltpu.VMEM((5 * 26, 8, LANES), F32),
            pltpu.VMEM((RANKS * 6, 8, LANES), F32),
            pltpu.VMEM((132, 8, LANES), F32),
        ],
        name="owner",
    )(owned.reshape(peers * ROWS_IN, LANES), partner)
    back = lax.all_to_all(returned.reshape(peers, ROWS_BACK, LANES), "obs", 0, 0, tiled=True)
    blocks = pl.pallas_call(
        camera_kernel,
        out_shape=jax.ShapeDtypeStruct((8 * BLOCK, LANES), F32),
        scratch_shapes=[
            pltpu.VMEM((SIDE, 2 * SLOTS), BF16),
            pltpu.VMEM((SIDE, 2 * SLOTS), BF16),
            pltpu.VMEM((SIDE, 2 * SLOTS), BF16),
            pltpu.VMEM((SIDE, 2 * SLOTS), BF16),
            pltpu.VMEM((SIDE, LANES), F32),
            pltpu.VMEM((4 * ROWS_BACK, LANES), F32),
        ],
        name="camera",
    )(back.reshape(peers * ROWS_BACK, LANES), own, pair_slot)
    parts = lax.all_to_all(blocks.reshape(8, BLOCK, LANES), "row", 0, 0, tiled=True)
    return pl.pallas_call(
        final_kernel,
        out_shape=(
            jax.ShapeDtypeStruct((81, CAM_ROW), F32),
            jax.ShapeDtypeStruct((9, CAM_ROW), F32),
            jax.ShapeDtypeStruct((81, CAM_ROW * NBR), F32),
        ),
        scratch_shapes=[pltpu.VMEM((BLOCK, LANES), F32), pltpu.VMEM((SIDE, LANES), F32), pltpu.VMEM((264, LANES), F32)],
        name="final",
    )(parts.reshape(8 * BLOCK, LANES))


def solution(mesh):
    return jax.shard_map(
        on_device,
        mesh=mesh,
        in_specs=(
            P(None, ("obs", "row")),
            P(None, ("obs", "row")),
            P(None, ("obs", "row")),
            P(("obs", "row")),
            P(("obs", "row")),
            P(("obs", "row")),
            P(None, ("obs", "row")),
            P(None, ("obs", "row")),
        ),
        out_specs=(P(None, ("obs", "row")), P(None, ("obs", "row")), P(None, ("obs", "row"))),
        check_vma=False,
    )
```

```python
import functools

import jax
import jax.numpy as jnp
from jax import lax
from jax.experimental import pallas as pl
from jax.experimental.pallas import tpu as pltpu
from jax.sharding import PartitionSpec as P

CAM_ROW = 16
NBR = 14
RANKS = 7
LANES = 128
GROUP = 32
SLOTS = 1024
CHUNKS = SLOTS // LANES
ROWS_IN = 8
ROWS_BACK = 40
USED_BACK = 33
SIDE = 144
BLOCK = 176
damping = 1.0
COST = pl.CostEstimate(flops=4_000_000_000, bytes_accessed=4_000_000, transcendentals=0)
F32 = jnp.float32
BF16 = jnp.bfloat16


def lane_groups():
    return lax.broadcasted_iota(jnp.int32, (8, LANES), 1) // GROUP


def regroup(parts, group, sign):
    outs = []
    for a in range(4):
        out = parts[a]
        for b in range(4):
            if b != a:
                out = jnp.where(group == b, pltpu.roll(parts[b], ((b - a) * GROUP) % LANES, 1), out)
        outs.append(out)
    return outs


def pack_kernel(jc, jp, err, cam, order, msg, own, rows):
    rows[0:18, :] = jc[...]
    rows[18:24, :] = jp[...]
    rows[24:26, :] = err[...]
    rows[26:27, :] = cam[...].astype(F32)
    rows[27:32, :] = jnp.zeros((5, SLOTS), F32)
    group = lane_groups()

    def chunk(d, _):
        at = pl.multiple_of(d * LANES, LANES)
        idx = jnp.broadcast_to(order[0:1, pl.ds(at, LANES)], (8, LANES))
        part = idx // LANES
        lane = idx % LANES
        tiles = []
        for t in range(4):
            acc = jnp.zeros((8, LANES), F32)
            for s in range(CHUNKS):
                got = jnp.take_along_axis(rows[t * 8 : t * 8 + 8, s * LANES : (s + 1) * LANES], lane, axis=1)
                acc = jnp.where(part == s, got, acc)
            own[t * 8 : t * 8 + 8, pl.ds(at, LANES)] = acc
            tiles.append(acc)
        for m, tile in enumerate(regroup(tiles, group, 1)):
            msg[pl.ds(pl.multiple_of((d * 4 + m) * ROWS_IN, 8), 8), :] = tile
        return 0

    lax.fori_loop(0, CHUNKS, chunk, 0)


ROLLS = (0, 1, 2, 6, 7)


def owner_kernel(owned, partner, msg, slots, turned, near, back):
    group = lane_groups()
    for r in range(8):
        slots[pl.ds(r, RANKS, stride=8), :] = partner[:, r * LANES : (r + 1) * LANES]
    for row in range(ROWS_IN):
        ins = [owned[pl.ds(m * ROWS_IN + row, 8, stride=4 * ROWS_IN), :] for m in range(4)]
        for t, tile in enumerate(regroup(ins, group, 1)):
            u = t * 8 + row
            if u < 26:
                for n, d in enumerate(ROLLS):
                    turned[n * 26 + u] = tile if d == 0 else pltpu.roll(tile, 8 - d, 0)
    here = lax.broadcasted_iota(jnp.int32, (8, LANES), 0)
    self_slot = here * LANES + lax.broadcasted_iota(jnp.int32, (8, LANES), 1)

    def picks(k):
        idx = slots[pl.ds(pl.multiple_of(k * 8, 8), 8), :]
        step = (idx // LANES - here) % 8
        return idx != self_slot, idx % LANES, [step == d for d in ROLLS]

    def pick(u, lane, masks):
        out = jnp.take_along_axis(turned[u], lane, axis=1)
        for n in range(1, len(ROLLS)):
            out = jnp.where(masks[n], jnp.take_along_axis(turned[n * 26 + u], lane, axis=1), out)
        return out

    def normal(p, e):
        out = []
        for a in range(3):
            for b in range(a, 3):
                out.append(p[a] * p[b] + p[3 + a] * p[3 + b])
        for a in range(3):
            out.append(p[a] * e[0] + p[3 + a] * e[1])
        return out

    mine = [turned[18 + n] for n in range(8)]

    def first(k, total):
        valid, lane, masks = picks(k)
        got = [jnp.where(valid, pick(18 + n, lane, masks), 0.0) for n in range(8)]
        for n in range(6):
            near[k * 6 + n] = got[n]
        return tuple(x + y for x, y in zip(total, normal(got[:6], got[6:])))

    v00, v01, v02, v11, v12, v22, b0, b1, b2 = lax.fori_loop(0, RANKS, first, tuple(normal(mine[:6], mine[6:])))
    i0 = 1.0 / jnp.sqrt(v00 + damping)
    l10 = v01 * i0
    l20 = v02 * i0
    i1 = 1.0 / jnp.sqrt(v11 + damping - l10 * l10)
    l21 = (v12 - l20 * l10) * i1
    i2 = 1.0 / jnp.sqrt(v22 + damping - l20 * l20 - l21 * l21)

    def forward(x0, x1, x2):
        y0 = x0 * i0
        y1 = (x1 - l10 * y0) * i1
        y2 = (x2 - l20 * y0 - l21 * y1) * i2
        return y0, y1, y2

    def inner(x, y):
        return x[0] * y[0] + x[1] * y[1] + x[2] * y[2]

    h = forward(b0, b1, b2)
    g = [forward(*mine[0:3]), forward(*mine[3:6])]
    back[126] = inner(g[0], g[0])
    back[127] = inner(g[0], g[1])
    back[128] = inner(g[1], g[1])
    back[129] = inner(g[0], h)
    back[130] = inner(g[1], h)
    back[131] = jnp.zeros((8, LANES), F32)

    def second(k, _):
        valid, lane, masks = picks(k)
        p = [near[k * 6 + n] for n in range(6)]
        o = [forward(*p[0:3]), forward(*p[3:6])]
        mix = [[-inner(g[a], o[b]) for b in range(2)] for a in range(2)]
        for q in range(9):
            c0 = pick(q, lane, masks)
            c1 = pick(9 + q, lane, masks)
            for a in range(2):
                back[k * 18 + a * 9 + q] = mix[a][0] * c0 + mix[a][1] * c1
        return 0

    lax.fori_loop(0, RANKS, second, 0)

    def emit(row, _):
        tiles = [back[row * 4 + t] for t in range(4)]
        for m, tile in enumerate(regroup(tiles, group, 1)):
            msg[pl.ds(m * ROWS_BACK + row, 8, stride=4 * ROWS_BACK), :] = tile
        return 0

    lax.fori_loop(0, USED_BACK, emit, 0)


def build_right(back, own, pair_slot, right_hi, right_lo, flat):
    group = lane_groups()
    low = lax.broadcasted_iota(jnp.int32, (8, LANES), 0)
    offsets = [low, low + 8]

    def chunk(d, _):
        at = pl.multiple_of(d * LANES, LANES)
        for b in range(ROWS_BACK // 8):
            ins = [back[pl.ds(pl.multiple_of((d * 4 + m) * ROWS_BACK + b * 8, 8), 8), :] for m in range(4)]
            for t, tile in enumerate(regroup(ins, group, 1)):
                flat[t * ROWS_BACK + b * 8 : t * ROWS_BACK + b * 8 + 8, :] = tile

        def spread(u):
            row = (u % 4) * ROWS_BACK + u // 4
            return jnp.broadcast_to(flat[row : row + 1, :], (8, LANES))

        def mine(u):
            return jnp.broadcast_to(own[u : u + 1, pl.ds(at, LANES)], (8, LANES))

        cam = mine(26).astype(jnp.int32)
        hits = []
        for k in range(RANKS):
            slot = jnp.broadcast_to(pair_slot[k : k + 1, pl.ds(at, LANES)], (8, LANES))
            o = jnp.where(slot == CAM_ROW * 8 * NBR, -1, slot - cam * NBR)
            hits.append([o == off for off in offsets])
        m00, m01, m11 = spread(126), spread(127), spread(128)
        grad = [mine(24) - spread(129), mine(25) - spread(130)]
        for q in range(9):
            c0, c1 = mine(q), mine(9 + q)
            diag = [c0 - m00 * c0 - m01 * c1, c1 - m01 * c0 - m11 * c1]
            for i in range(2):
                halves = [jnp.zeros((8, LANES), F32), jnp.where(low == 6, diag[i], 0.0)]
                if q == 0:
                    halves[1] = jnp.where(low == 7, grad[i], halves[1])
                for k in range(RANKS):
                    n = spread(k * 18 + i * 9 + q)
                    halves = [x + jnp.where(hit, n, 0.0) for x, hit in zip(halves, hits[k])]
                value = jnp.concatenate(halves, axis=0)
                hi = value.astype(BF16)
                at2 = pl.multiple_of(d * 2 * LANES + i * LANES, LANES)
                right_hi[q * 16 : q * 16 + 16, pl.ds(at2, LANES)] = hi
                right_lo[q * 16 : q * 16 + 16, pl.ds(at2, LANES)] = (value - hi.astype(F32)).astype(BF16)
        return 0

    lax.fori_loop(0, CHUNKS, chunk, 0)


def dot_t(x, y):
    return lax.dot_general(x, y, (((1,), (1,)), ((), ())), preferred_element_type=F32)


def build_block(dest, own, right_hi, right_lo, left_hi, left_lo, wide, out):
    low = lax.broadcasted_iota(jnp.int32, (16, LANES), 0).astype(F32) + (dest * CAM_ROW).astype(F32)

    def chunk(d, _):
        at = pl.multiple_of(d * LANES, LANES)
        hit = jnp.broadcast_to(own[26:27, pl.ds(at, LANES)], (16, LANES)) == low
        for i in range(2):
            at2 = pl.multiple_of(d * 2 * LANES + i * LANES, LANES)
            for p in range(9):
                u = i * 9 + p
                value = jnp.broadcast_to(own[u : u + 1, pl.ds(at, LANES)], (16, LANES))
                value = jnp.where(hit, value, 0.0)
                hi = value.astype(BF16)
                left_hi[p * 16 : p * 16 + 16, pl.ds(at2, LANES)] = hi
                left_lo[p * 16 : p * 16 + 16, pl.ds(at2, LANES)] = (value - hi.astype(F32)).astype(BF16)
        return 0

    lax.fori_loop(0, CHUNKS, chunk, 0)
    total = dot_t(left_hi[...], right_hi[...]) + (
        dot_t(left_hi[...], right_lo[...]) + dot_t(left_lo[...], right_hi[...])
    )
    out[0:SIDE, :] = total[:, :LANES]
    wide[:, 0:16] = total[:, LANES:]
    lane = lax.broadcasted_iota(jnp.int32, (16, LANES), 1)
    tail = wide[0:16, :]
    for p in range(1, 8):
        tail = jnp.where(lane // 16 == p, pltpu.roll(wide[p * 16 : p * 16 + 16, :], p * 16, 1), tail)
    out[SIDE : SIDE + 16, :] = tail
    out[SIDE + 16 : BLOCK, :] = wide[128:144, :]


def first_kernel(row, back, own, pair_slot, plus, minus, right_hi, right_lo, left_hi, left_lo, wide, flat):
    build_right(back, own, pair_slot, right_hi, right_lo, flat)
    wide[...] = jnp.zeros((SIDE, LANES), F32)
    build_block((row[0] + 4) % 8, own, right_hi, right_lo, left_hi, left_lo, wide, plus)
    build_block((row[0] + 5) % 8, own, right_hi, right_lo, left_hi, left_lo, wide, minus)


def next_kernel(step, row, own, right_hi, right_lo, plus, minus, left_hi, left_lo, wide):
    wide[...] = jnp.zeros((SIDE, LANES), F32)
    build_block((row[0] + 4 - step) % 8, own, right_hi, right_lo, left_hi, left_lo, wide, plus)
    build_block((row[0] + 5 + step) % 8, own, right_hi, right_lo, left_hi, left_lo, wide, minus)


def final_kernel(own, plus, minus, hess, grad, pair, body, last, rows):
    body[...] = own[...] + (plus[...] + minus[...])
    for p in range(8):
        piece = body[SIDE : SIDE + 16, :]
        last[p * 16 : p * 16 + 16, :] = piece if p == 0 else pltpu.roll(piece, (LANES - p * 16) % LANES, 1)
    last[128:144, :] = body[SIDE + 16 : BLOCK, :]
    lane = lax.broadcasted_iota(jnp.int32, (9, LANES), 1)
    grads = jnp.zeros((9, LANES), F32)
    for q in range(9):
        halves = [jnp.zeros((9, LANES), F32), jnp.zeros((9, LANES), F32)]
        for c in range(CAM_ROW):
            ref, at = (body, q * 16) if q < 8 else (last, 0)
            x = ref[pl.ds(c, 9, stride=16), :]
            turn = pltpu.roll(x, (c * NBR - at) % LANES, 1)
            for half in range(2):
                lo, hi = c * NBR - half * LANES, (c + 1) * NBR - half * LANES
                if hi > 0 and lo < LANES:
                    halves[half] = jnp.where((lane >= lo) & (lane < hi), turn, halves[half])
            if q == 0:
                grads = jnp.where(lane == c, pltpu.roll(x, (c - at - 15) % LANES, 1), grads)
        for n, x in enumerate(halves):
            rows[pl.ds(n * 88 + q, 9, stride=9), :] = x
    pair[:, 0:LANES] = rows[0:81, :]
    pair[:, LANES : CAM_ROW * NBR] = rows[88:169, : CAM_ROW * NBR - LANES]
    lane = lax.broadcasted_iota(jnp.int32, (16, LANES), 1)
    diag = jnp.zeros((16, LANES), F32)
    for p in range(9):
        for q in range(9):
            ref, at = (body, q * 16) if q < 8 else (last, 0)
            x = ref[p * 16 : p * 16 + 16, :]
            diag = jnp.where(lane == p * 9 + q, pltpu.roll(x, (p * 9 + q - at - 14) % LANES, 1), diag)
    hess[...] = diag[:, :81]
    grad[...] = grads[:, :CAM_ROW]


def on_device(
    camera_jacobian, point_jacobian, residual, send_order, camera_of, track_of, partner, pair_slot
):
    peers = lax.axis_size("obs")
    msg, own = pl.pallas_call(
        pack_kernel,
        out_shape=(
            jax.ShapeDtypeStruct((peers * ROWS_IN, LANES), F32),
            jax.ShapeDtypeStruct((32, SLOTS), F32),
        ),
        scratch_shapes=[pltpu.VMEM((32, SLOTS), F32)],
        name="pack",
    )(camera_jacobian, point_jacobian, residual, camera_of.reshape(1, SLOTS), send_order.reshape(1, SLOTS))
    owned = lax.all_to_all(msg.reshape(peers, ROWS_IN, LANES), "obs", 0, 0, tiled=True)
    returned = pl.pallas_call(
        owner_kernel,
        out_shape=jax.ShapeDtypeStruct((peers * ROWS_BACK, LANES), F32),
        scratch_shapes=[
            pltpu.VMEM((RANKS * 8, LANES), jnp.int32),
            pltpu.VMEM((5 * 26, 8, LANES), F32),
            pltpu.VMEM((RANKS * 6, 8, LANES), F32),
            pltpu.VMEM((132, 8, LANES), F32),
        ],
        name="owner",
    )(owned.reshape(peers * ROWS_IN, LANES), partner)
    back = lax.all_to_all(returned.reshape(peers, ROWS_BACK, LANES), "obs", 0, 0, tiled=True)
    row = lax.axis_index("row").astype(jnp.int32).reshape(1)
    here = pl.BlockSpec(memory_space=pltpu.VMEM)
    scalar = pl.BlockSpec(memory_space=pltpu.SMEM)
    block = jax.ShapeDtypeStruct((BLOCK, LANES), F32)
    side = jax.ShapeDtypeStruct((SIDE, 2 * SLOTS), BF16)
    left = [pltpu.VMEM((SIDE, 2 * SLOTS), BF16), pltpu.VMEM((SIDE, 2 * SLOTS), BF16), pltpu.VMEM((SIDE, LANES), F32)]
    params = pltpu.CompilerParams(vmem_limit_bytes=16 << 20)
    plus, minus, right_hi, right_lo = pl.pallas_call(
        first_kernel,
        in_specs=[scalar, here, here, here],
        out_shape=(block, block, side, side),
        scratch_shapes=left + [pltpu.VMEM((4 * ROWS_BACK, LANES), F32)],
        compiler_params=params,
        cost_estimate=COST,
        name="camera_0",
    )(row, back.reshape(peers * ROWS_BACK, LANES), own, pair_slot)
    for step in range(1, 4):
        plus = lax.ppermute(plus, "row", [(n, (n + 1) % 8) for n in range(8)])
        minus = lax.ppermute(minus, "row", [(n, (n - 1) % 8) for n in range(8)])
        more_plus, more_minus = pl.pallas_call(
            functools.partial(next_kernel, step),
            in_specs=[scalar, here, here, here],
            out_shape=(block, block),
            scratch_shapes=left,
            compiler_params=params,
            cost_estimate=COST,
            name=f"camera_{step}",
        )(row, own, right_hi, right_lo)
        plus = plus + more_plus
        if step < 3:
            minus = minus + more_minus
    plus = lax.ppermute(plus, "row", [(n, (n + 1) % 8) for n in range(8)])
    hess, grad, pair = pl.pallas_call(
        final_kernel,
        out_shape=(
            jax.ShapeDtypeStruct((CAM_ROW, 81), F32),
            jax.ShapeDtypeStruct((9, CAM_ROW), F32),
            jax.ShapeDtypeStruct((81, CAM_ROW * NBR), F32),
        ),
        scratch_shapes=[
            pltpu.VMEM((BLOCK, LANES), F32),
            pltpu.VMEM((SIDE, LANES), F32),
            pltpu.VMEM((176, LANES), F32),
        ],
        compiler_params=params,
        name="final",
    )(more_minus, plus, minus)
    return hess.T, grad, pair


def solution(mesh):
    return jax.shard_map(
        on_device,
        mesh=mesh,
        in_specs=(
            P(None, ("obs", "row")),
            P(None, ("obs", "row")),
            P(None, ("obs", "row")),
            P(("obs", "row")),
            P(("obs", "row")),
            P(("obs", "row")),
            P(None, ("obs", "row")),
            P(None, ("obs", "row")),
        ),
        out_specs=(P(None, ("obs", "row")), P(None, ("obs", "row")), P(None, ("obs", "row"))),
        check_vma=False,
    )
```

```python
import functools

import jax
import jax.numpy as jnp
from jax import lax
from jax.experimental import pallas as pl
from jax.experimental.pallas import tpu as pltpu
from jax.sharding import PartitionSpec as P


CAM_ROW = 16
NBR = 14
RANKS = 7
LANES = 128
GROUP = 32
SLOTS = 1024
CHUNKS = SLOTS // LANES
ROWS_IN = 8
ROWS_BACK = 33
SIDE = 144
BLOCK = 176
damping = 1.0
COST = pl.CostEstimate(flops=4_000_000_000, bytes_accessed=4_000_000, transcendentals=0)
PARAMS = pltpu.CompilerParams(vmem_limit_bytes=16 << 20)
F32 = jnp.float32
BF16 = jnp.bfloat16
TILE = (8, LANES)


def lane_groups():
    return lax.broadcasted_iota(jnp.int32, TILE, 1) // GROUP


def regroup(parts, group):
    outs = []
    for a in range(4):
        out = parts[a]
        for b in range(4):
            if b != a:
                out = jnp.where(group == b, pltpu.roll(parts[b], ((b - a) * GROUP) % LANES, 1), out)
        outs.append(out)
    return outs


def ordered(rows, order, d, t):
    idx = jnp.broadcast_to(order[0:1, d * LANES : (d + 1) * LANES], TILE)
    part = idx // LANES
    lane = idx % LANES
    out = None
    for s in range(CHUNKS):
        got = jnp.take_along_axis(rows[t * 8 : t * 8 + 8, s * LANES : (s + 1) * LANES], lane, axis=1)
        out = got if out is None else jnp.where(part == s, got, out)
    return out


def fill_rows(jc, jp, err, cam, rows):
    rows[0:18, :] = jc[...]
    rows[18:24, :] = jp[...]
    rows[24:26, :] = err[...]
    rows[26:27, :] = cam[...].astype(F32)
    rows[27:32, :] = jnp.zeros((5, SLOTS), F32)


def pack_kernel(jc, jp, err, cam, order, msg, rows):
    fill_rows(jc, jp, err, cam, rows)
    group = lane_groups()
    for d in range(CHUNKS):
        tiles = [ordered(rows, order, d, t) for t in range(4)]
        for m, tile in enumerate(regroup(tiles, group)):
            msg[(d * 4 + m) * ROWS_IN : (d * 4 + m) * ROWS_IN + 8, :] = tile


def own_kernel(jc, jp, err, cam, order, own, split, rows):
    fill_rows(jc, jp, err, cam, rows)
    for d in range(CHUNKS):
        cols = slice(d * LANES, (d + 1) * LANES)
        for t in range(4):
            value = ordered(rows, order, d, t)
            own[t * 8 : t * 8 + 8, cols] = value
            if t < 3:
                hi = value.astype(BF16).astype(F32)
                split[t * 8 : t * 8 + 8, cols] = hi
                split[24 + t * 8 : 32 + t * 8, cols] = (value - hi).astype(BF16).astype(F32)


def owner_kernel(owned, partner, msg, slots, turned, near, mixed, back):
    group = lane_groups()
    for r in range(8):
        slots[pl.ds(r, RANKS, stride=8), :] = partner[:, r * LANES : (r + 1) * LANES]
    for row in range(ROWS_IN):
        ins = [owned[pl.ds(m * ROWS_IN + row, 8, stride=4 * ROWS_IN), :] for m in range(4)]
        for t, tile in enumerate(regroup(ins, group)):
            u = t * 8 + row
            if u >= 26:
                continue
            turned[u] = tile
            for b in range(4):
                lanes = pltpu.roll(tile, LANES - b * GROUP, 1) if b else tile
                up = [lanes, pltpu.roll(lanes, 7, 0), pltpu.roll(lanes, 6, 0)] if b else [lanes, pltpu.roll(lanes, 7, 0)]
                for a in range(2):
                    j = a * 4 + b
                    if j:
                        here = jnp.where(group < 4 - b, up[a], up[a + 1]) if b else up[a]
                        turned[j * 52 + u] = here
                        turned[j * 52 + 26 + u] = pltpu.roll(here, 2, 0)
    source = lax.broadcasted_iota(jnp.int32, TILE, 0) * 4 + group
    ranks, words = [], []
    for k in range(RANKS):
        idx = slots[k * 8 : k * 8 + 8, :]
        apart = (idx // GROUP - source) & 31
        ranks.append(apart & 7)
        words.append((idx & 31) + jnp.where(apart < 16, GROUP, 0))

    def picks(j):
        word = jnp.full(TILE, -1, jnp.int32)
        for k in range(RANKS):
            word = jnp.where(ranks[k] == j, words[k], word)
        return word >= 0, group * GROUP + (word & 31), word >= GROUP

    def pick(u, j, lane, ahead):
        front = jnp.take_along_axis(turned[j * 52 + u], lane, axis=1)
        behind = jnp.take_along_axis(turned[j * 52 + 26 + u], lane, axis=1)
        return jnp.where(ahead, front, behind)

    def normal(p, e):
        out = []
        for a in range(3):
            for b in range(a, 3):
                out.append(p[a] * p[b] + p[3 + a] * p[3 + b])
        for a in range(3):
            out.append(p[a] * e[0] + p[3 + a] * e[1])
        return out

    mine = [turned[18 + n] for n in range(8)]
    total = normal(mine[:6], mine[6:])
    for j in range(1, 8):
        valid, lane, ahead = picks(j)
        got = [jnp.where(valid, pick(18 + n, j, lane, ahead), 0.0) for n in range(8)]
        for n in range(6):
            near[(j - 1) * 6 + n] = got[n]
        total = [x + y for x, y in zip(total, normal(got[:6], got[6:]))]
    v00, v01, v02, v11, v12, v22, b0, b1, b2 = total
    i0 = 1.0 / jnp.sqrt(v00 + damping)
    l10 = v01 * i0
    l20 = v02 * i0
    i1 = 1.0 / jnp.sqrt(v11 + damping - l10 * l10)
    l21 = (v12 - l20 * l10) * i1
    i2 = 1.0 / jnp.sqrt(v22 + damping - l20 * l20 - l21 * l21)

    def forward(x0, x1, x2):
        y0 = x0 * i0
        y1 = (x1 - l10 * y0) * i1
        y2 = (x2 - l20 * y0 - l21 * y1) * i2
        return y0, y1, y2

    def inner(x, y):
        return x[0] * y[0] + x[1] * y[1] + x[2] * y[2]

    h = forward(b0, b1, b2)
    g = [forward(*mine[0:3]), forward(*mine[3:6])]
    back[126] = inner(g[0], g[0])
    back[127] = inner(g[0], g[1])
    back[128] = inner(g[1], g[1])
    back[129] = inner(g[0], h)
    back[130] = inner(g[1], h)
    back[131] = jnp.zeros(TILE, F32)

    for j in range(1, 8):
        _, lane, ahead = picks(j)
        p = [near[(j - 1) * 6 + n] for n in range(6)]
        o = [forward(*p[0:3]), forward(*p[3:6])]
        mix = [[-inner(g[a], o[b]) for b in range(2)] for a in range(2)]
        for q in range(9):
            c0 = pick(q, j, lane, ahead)
            c1 = pick(9 + q, j, lane, ahead)
            for a in range(2):
                mixed[(j - 1) * 18 + a * 9 + q] = mix[a][0] * c0 + mix[a][1] * c1
    for k in range(RANKS):
        hits = [ranks[k] == j for j in range(1, 8)]
        for n in range(18):
            out = jnp.zeros(TILE, F32)
            for j in range(7):
                out = jnp.where(hits[j], mixed[j * 18 + n], out)
            back[k * 18 + n] = out
    for row in range(ROWS_BACK):
        tiles = [back[row * 4 + t] for t in range(4)]
        for m, tile in enumerate(regroup(tiles, group)):
            msg[pl.ds(m * ROWS_BACK + row, 8, stride=4 * ROWS_BACK), :] = tile


def build_right(back, own, pair_slot, right_hi, right_lo, flat):
    group = lane_groups()
    low = lax.broadcasted_iota(jnp.int32, TILE, 0)
    for row in range(ROWS_BACK):
        ins = [back[pl.ds(m * ROWS_BACK + row, 8, stride=4 * ROWS_BACK), :] for m in range(4)]
        for t, tile in enumerate(regroup(ins, group)):
            flat[(row * 4 + t) * 8 : (row * 4 + t) * 8 + 8, :] = tile
    for d in range(CHUNKS):
        cols = slice(d * LANES, (d + 1) * LANES)

        def spread(u):
            return jnp.broadcast_to(flat[u * 8 + d : u * 8 + d + 1, :], TILE)

        def mine(u):
            return jnp.broadcast_to(own[u : u + 1, cols], TILE)

        cam = mine(26).astype(jnp.int32)
        m00, m01, m11 = spread(126), spread(127), spread(128)
        grad = [mine(24) - spread(129), mine(25) - spread(130)]
        total = {}
        for q in range(9):
            c0, c1 = mine(q), mine(9 + q)
            diag = [c0 - m00 * c0 - m01 * c1, c1 - m01 * c0 - m11 * c1]
            for i in range(2):
                tail = jnp.where(low == 6, diag[i], 0.0)
                if q == 0:
                    tail = jnp.where(low == 7, grad[i], tail)
                total[q, i, 1] = tail
        for k in range(RANKS):
            slot = jnp.broadcast_to(pair_slot[k : k + 1, cols], TILE)
            o = jnp.where(slot == CAM_ROW * 8 * NBR, -1, slot - cam * NBR)
            hits = [o == low, o == low + 8]
            for q in range(9):
                for i in range(2):
                    n = spread(k * 18 + i * 9 + q)
                    for side in range(2):
                        term = jnp.where(hits[side], n, 0.0)
                        total[q, i, side] = term if (q, i, side) not in total else total[q, i, side] + term
        for q in range(9):
            for i in range(2):
                value = jnp.concatenate([total[q, i, 0], total[q, i, 1]], axis=0)
                hi = value.astype(BF16)
                at = slice((d * 2 + i) * LANES, (d * 2 + i + 1) * LANES)
                right_hi[q * 16 : q * 16 + 16, at] = hi
                right_lo[q * 16 : q * 16 + 16, at] = (value - hi.astype(F32)).astype(BF16)


def dot_t(x, y):
    return lax.dot_general(x, y, (((1,), (1,)), ((), ())), preferred_element_type=F32)


def build_blocks(dests, own, split, right_hi, right_lo, left, wide, outs):
    count = len(dests)
    low = lax.broadcasted_iota(jnp.int32, TILE, 0)
    bases = [(dest * CAM_ROW + low).astype(F32) for dest in dests]
    for d in range(CHUNKS):
        cols = slice(d * LANES, (d + 1) * LANES)
        cam = jnp.broadcast_to(own[26:27, cols], TILE)
        hits = [[cam == base, cam == base + 8.0] for base in bases]
        for i in range(2):
            at = slice((d * 2 + i) * LANES, (d * 2 + i + 1) * LANES)
            for p in range(9):
                for part in range(2):
                    u = part * 24 + i * 9 + p
                    value = jnp.broadcast_to(split[u : u + 1, cols], TILE)
                    for n in range(count):
                        at_row = (part * count + n) * SIDE + p * 16
                        pair = [jnp.where(hit, value, 0.0) for hit in hits[n]]
                        left[at_row : at_row + 16, at] = jnp.concatenate(pair, axis=0).astype(BF16)
    size = count * SIDE
    by_hi = dot_t(left[0 : 2 * size, :], right_hi[...])
    by_lo = dot_t(left[0:size, :], right_lo[...])
    total = by_hi[0:size] + (by_hi[size : 2 * size] + by_lo)
    lane = lax.broadcasted_iota(jnp.int32, (16, LANES), 1)
    for n, out in enumerate(outs):
        block = total[n * SIDE : (n + 1) * SIDE]
        out[0:SIDE, :] = block[:, :LANES]
        wide[:, 0:16] = block[:, LANES:]
        tail = wide[0:16, :]
        for p in range(1, 8):
            tail = jnp.where(lane // 16 == p, pltpu.roll(wide[p * 16 : p * 16 + 16, :], p * 16, 1), tail)
        out[SIDE : SIDE + 16, :] = tail
        out[SIDE + 16 : BLOCK, :] = wide[128:144, :]


def first_kernel(row, back, own, split, pair_slot, block, right_hi, right_lo, left, wide, flat):
    build_right(back, own, pair_slot, right_hi, right_lo, flat)
    wide[...] = jnp.zeros((SIDE, LANES), F32)
    build_blocks([(row[0] + 4) % 8], own, split, right_hi, right_lo, left, wide, [block])


def next_kernel(shifts, row, own, split, right_hi, right_lo, *rest):
    outs, (left, wide) = rest[: len(shifts)], rest[len(shifts) :]
    wide[...] = jnp.zeros((SIDE, LANES), F32)
    build_blocks([(row[0] + s) % 8 for s in shifts], own, split, right_hi, right_lo, left, wide, outs)


def final_kernel(own, plus1, minus1, plus2, minus2, hess, grad, pair, body, last, rows):
    body[...] = own[...] + ((plus1[...] + minus1[...]) + (plus2[...] + minus2[...]))
    for p in range(8):
        piece = body[SIDE : SIDE + 16, :]
        last[p * 16 : p * 16 + 16, :] = piece if p == 0 else pltpu.roll(piece, (LANES - p * 16) % LANES, 1)
    last[128:144, :] = body[SIDE + 16 : BLOCK, :]
    lane = lax.broadcasted_iota(jnp.int32, (9, LANES), 1)
    grads = jnp.zeros((9, LANES), F32)
    for q in range(9):
        halves = [jnp.zeros((9, LANES), F32), jnp.zeros((9, LANES), F32)]
        for c in range(CAM_ROW):
            ref, at = (body, q * 16) if q < 8 else (last, 0)
            x = ref[pl.ds(c, 9, stride=16), :]
            turn = pltpu.roll(x, (c * NBR - at) % LANES, 1)
            for half in range(2):
                lo, hi = c * NBR - half * LANES, (c + 1) * NBR - half * LANES
                if hi > 0 and lo < LANES:
                    halves[half] = jnp.where((lane >= lo) & (lane < hi), turn, halves[half])
            if q == 0:
                grads = jnp.where(lane == c, pltpu.roll(x, (c - at - 15) % LANES, 1), grads)
        for n, x in enumerate(halves):
            rows[pl.ds(n * 88 + q, 9, stride=9), :] = x
    pair[:, 0:LANES] = rows[0:81, :]
    pair[:, LANES : CAM_ROW * NBR] = rows[88:169, : CAM_ROW * NBR - LANES]
    lane = lax.broadcasted_iota(jnp.int32, (16, LANES), 1)
    diag = jnp.zeros((16, LANES), F32)
    for p in range(9):
        for q in range(9):
            ref, at = (body, q * 16) if q < 8 else (last, 0)
            x = ref[p * 16 : p * 16 + 16, :]
            diag = jnp.where(lane == p * 9 + q, pltpu.roll(x, (p * 9 + q - at - 14) % LANES, 1), diag)
    hess[...] = diag[:, :81]
    grad[...] = grads[:, :CAM_ROW]


def on_device(
    camera_jacobian, point_jacobian, residual, send_order, camera_of, track_of, partner, pair_slot
):
    peers = lax.axis_size("obs")
    row = lax.axis_index("row").astype(jnp.int32).reshape(1)
    vmem = pl.BlockSpec(memory_space=pltpu.VMEM)
    smem = pl.BlockSpec(memory_space=pltpu.SMEM)
    raw = (camera_jacobian, point_jacobian, residual, camera_of.reshape(1, SLOTS), send_order.reshape(1, SLOTS))
    msg = pl.pallas_call(
        pack_kernel,
        out_shape=jax.ShapeDtypeStruct((peers * ROWS_IN, LANES), F32),
        scratch_shapes=[pltpu.VMEM((32, SLOTS), F32)],
        name="pack",
    )(*raw)
    owned = lax.all_to_all(msg.reshape(peers, ROWS_IN, LANES), "obs", 0, 0, tiled=True)
    returned = pl.pallas_call(
        owner_kernel,
        out_shape=jax.ShapeDtypeStruct((peers * ROWS_BACK, LANES), F32),
        scratch_shapes=[
            pltpu.VMEM((RANKS * 8, LANES), jnp.int32),
            pltpu.VMEM((8 * 52, 8, LANES), F32),
            pltpu.VMEM((RANKS * 6, 8, LANES), F32),
            pltpu.VMEM((RANKS * 18, 8, LANES), F32),
            pltpu.VMEM((132, 8, LANES), F32),
        ],
        compiler_params=PARAMS,
        name="owner",
    )(owned.reshape(peers * ROWS_IN, LANES), partner)
    back = lax.all_to_all(returned.reshape(peers, 1, ROWS_BACK * LANES), "obs", 0, 0, tiled=True)
    block = jax.ShapeDtypeStruct((BLOCK, LANES), F32)
    side = jax.ShapeDtypeStruct((SIDE, 2 * SLOTS), BF16)
    own, split = pl.pallas_call(
        own_kernel,
        out_shape=(jax.ShapeDtypeStruct((32, SLOTS), F32), jax.ShapeDtypeStruct((48, SLOTS), F32)),
        scratch_shapes=[pltpu.VMEM((32, SLOTS), F32)],
        compiler_params=PARAMS,
        cost_estimate=COST,
        name="own",
    )(*raw)

    def scratch(count):
        return [pltpu.VMEM((2 * count * SIDE, 2 * SLOTS), BF16), pltpu.VMEM((SIDE, LANES), F32)]

    far, right_hi, right_lo = pl.pallas_call(
        first_kernel,
        in_specs=[smem, vmem, vmem, vmem, vmem],
        out_shape=(block, side, side),
        scratch_shapes=scratch(1) + [pltpu.VMEM((132 * 8, LANES), F32)],
        compiler_params=PARAMS,
        cost_estimate=COST,
        name="camera_0",
    )(row, back.reshape(peers * ROWS_BACK, LANES), own, split, pair_slot)

    def blocks(shifts):
        return pl.pallas_call(
            functools.partial(next_kernel, shifts),
            in_specs=[smem, vmem, vmem, vmem, vmem],
            out_shape=(block,) * len(shifts),
            scratch_shapes=scratch(len(shifts)),
            compiler_params=PARAMS,
            cost_estimate=COST,
        )(row, own, split, right_hi, right_lo)

    def shift(x, by):
        return lax.ppermute(x, "row", [(n, (n + by) % 8) for n in range(8)])

    far = shift(far, 2)
    plus, minus = blocks((3, 5))
    plus, minus = shift(plus, 1), shift(minus, -1)
    plus2, minus2 = blocks((2, 6))
    plus1, minus1 = blocks((1, 7))
    plus2 = shift(plus2 + (plus + far), 2)
    minus2 = shift(minus2 + minus, -2)
    plus1, minus1 = shift(plus1, 1), shift(minus1, -1)
    (kept,) = blocks((0,))
    hess, grad, pair = pl.pallas_call(
        final_kernel,
        out_shape=(
            jax.ShapeDtypeStruct((CAM_ROW, 81), F32),
            jax.ShapeDtypeStruct((9, CAM_ROW), F32),
            jax.ShapeDtypeStruct((81, CAM_ROW * NBR), F32),
        ),
        scratch_shapes=[
            pltpu.VMEM((BLOCK, LANES), F32),
            pltpu.VMEM((SIDE, LANES), F32),
            pltpu.VMEM((176, LANES), F32),
        ],
        compiler_params=PARAMS,
        name="final",
    )(kept, plus1, minus1, plus2, minus2)
    return hess.T, grad, pair


def solution(mesh):
    return jax.shard_map(
        on_device,
        mesh=mesh,
        in_specs=(
            P(None, ("obs", "row")),
            P(None, ("obs", "row")),
            P(None, ("obs", "row")),
            P(("obs", "row")),
            P(("obs", "row")),
            P(("obs", "row")),
            P(None, ("obs", "row")),
            P(None, ("obs", "row")),
        ),
        out_specs=(P(None, ("obs", "row")), P(None, ("obs", "row")), P(None, ("obs", "row"))),
        check_vma=False,
    )
```

```python
import functools

import jax
import jax.numpy as jnp
from jax import lax
from jax.experimental import pallas as pl
from jax.experimental.pallas import tpu as pltpu
from jax.sharding import PartitionSpec as P


CAM_ROW = 16
NBR = 14
RANKS = 7
LANES = 128
GROUP = 32
SLOTS = 1024
CHUNKS = SLOTS // LANES
ROWS_IN = 8
ROWS_BACK = 33
SIDE = 144
BLOCK = 176
damping = 1.0
COST = pl.CostEstimate(flops=4_000_000_000, bytes_accessed=4_000_000, transcendentals=0)
PARAMS = pltpu.CompilerParams(vmem_limit_bytes=16 << 20)
F32 = jnp.float32
BF16 = jnp.bfloat16
TILE = (8, LANES)


def lane_groups():
    return lax.broadcasted_iota(jnp.int32, TILE, 1) // GROUP


def regroup(parts, group):
    outs = []
    for a in range(4):
        out = parts[a]
        for b in range(4):
            if b != a:
                out = jnp.where(group == b, pltpu.roll(parts[b], ((b - a) * GROUP) % LANES, 1), out)
        outs.append(out)
    return outs


def ordered(rows, order, d, t):
    idx = jnp.broadcast_to(order[0:1, d * LANES : (d + 1) * LANES], TILE)
    part = idx // LANES
    lane = idx % LANES
    out = None
    for s in range(CHUNKS):
        got = jnp.take_along_axis(rows[t * 8 : t * 8 + 8, s * LANES : (s + 1) * LANES], lane, axis=1)
        out = got if out is None else jnp.where(part == s, got, out)
    return out


def fill_rows(jc, jp, err, cam, rows):
    rows[0:18, :] = jc[...]
    rows[18:24, :] = jp[...]
    rows[24:26, :] = err[...]
    rows[26:27, :] = cam[...].astype(F32)
    rows[27:32, :] = jnp.zeros((5, SLOTS), F32)


def pack_kernel(*refs):
    sources, (msg, rows, *targets, sems) = refs[:5], refs[5:]
    copies = [pltpu.make_async_copy(x, y, sems.at[n]) for n, (x, y) in enumerate(zip(sources, targets))]
    for copy in copies:
        copy.start()
    for copy in copies:
        copy.wait()
    jc, jp, err, cam, order = targets
    fill_rows(jc, jp, err, cam, rows)
    group = lane_groups()
    for d in range(CHUNKS):
        tiles = [ordered(rows, order, d, t) for t in range(4)]
        for m, tile in enumerate(regroup(tiles, group)):
            msg[(d * 4 + m) * ROWS_IN : (d * 4 + m) * ROWS_IN + 8, :] = tile


def own_kernel(jc, jp, err, cam, order, own, split, rows):
    fill_rows(jc, jp, err, cam, rows)
    for d in range(CHUNKS):
        cols = slice(d * LANES, (d + 1) * LANES)
        for t in range(4):
            value = ordered(rows, order, d, t)
            own[t * 8 : t * 8 + 8, cols] = value
            if t < 3:
                hi = value.astype(BF16).astype(F32)
                split[t * 8 : t * 8 + 8, cols] = hi
                split[24 + t * 8 : 32 + t * 8, cols] = (value - hi).astype(BF16).astype(F32)


def owner_kernel(owned, partner, msg, slots, turned, near, mixed, back):
    group = lane_groups()
    for r in range(8):
        slots[pl.ds(r, RANKS, stride=8), :] = partner[:, r * LANES : (r + 1) * LANES]
    for row in range(ROWS_IN):
        ins = [owned[pl.ds(m * ROWS_IN + row, 8, stride=4 * ROWS_IN), :] for m in range(4)]
        for t, tile in enumerate(regroup(ins, group)):
            u = t * 8 + row
            if u >= 26:
                continue
            turned[u] = tile
            for b in range(4):
                lanes = pltpu.roll(tile, LANES - b * GROUP, 1) if b else tile
                up = [lanes, pltpu.roll(lanes, 7, 0), pltpu.roll(lanes, 6, 0)] if b else [lanes, pltpu.roll(lanes, 7, 0)]
                for a in range(2):
                    j = a * 4 + b
                    if j:
                        here = jnp.where(group < 4 - b, up[a], up[a + 1]) if b else up[a]
                        turned[j * 52 + u] = here
                        turned[j * 52 + 26 + u] = pltpu.roll(here, 2, 0)
    source = lax.broadcasted_iota(jnp.int32, TILE, 0) * 4 + group
    ranks, words = [], []
    for k in range(RANKS):
        idx = slots[k * 8 : k * 8 + 8, :]
        apart = (idx // GROUP - source) & 31
        ranks.append(apart & 7)
        words.append((idx & 31) + jnp.where(apart < 16, GROUP, 0))

    def picks(j):
        word = jnp.full(TILE, -1, jnp.int32)
        for k in range(RANKS):
            word = jnp.where(ranks[k] == j, words[k], word)
        return word >= 0, group * GROUP + (word & 31), word >= GROUP

    def pick(u, j, lane, ahead):
        front = jnp.take_along_axis(turned[j * 52 + u], lane, axis=1)
        behind = jnp.take_along_axis(turned[j * 52 + 26 + u], lane, axis=1)
        return jnp.where(ahead, front, behind)

    def normal(p, e):
        out = []
        for a in range(3):
            for b in range(a, 3):
                out.append(p[a] * p[b] + p[3 + a] * p[3 + b])
        for a in range(3):
            out.append(p[a] * e[0] + p[3 + a] * e[1])
        return out

    mine = [turned[18 + n] for n in range(8)]
    total = normal(mine[:6], mine[6:])
    for j in range(1, 8):
        valid, lane, ahead = picks(j)
        got = [jnp.where(valid, pick(18 + n, j, lane, ahead), 0.0) for n in range(8)]
        for n in range(6):
            near[(j - 1) * 6 + n] = got[n]
        total = [x + y for x, y in zip(total, normal(got[:6], got[6:]))]
    v00, v01, v02, v11, v12, v22, b0, b1, b2 = total
    i0 = 1.0 / jnp.sqrt(v00 + damping)
    l10 = v01 * i0
    l20 = v02 * i0
    i1 = 1.0 / jnp.sqrt(v11 + damping - l10 * l10)
    l21 = (v12 - l20 * l10) * i1
    i2 = 1.0 / jnp.sqrt(v22 + damping - l20 * l20 - l21 * l21)

    def forward(x0, x1, x2):
        y0 = x0 * i0
        y1 = (x1 - l10 * y0) * i1
        y2 = (x2 - l20 * y0 - l21 * y1) * i2
        return y0, y1, y2

    def inner(x, y):
        return x[0] * y[0] + x[1] * y[1] + x[2] * y[2]

    h = forward(b0, b1, b2)
    g = [forward(*mine[0:3]), forward(*mine[3:6])]
    back[126] = inner(g[0], g[0])
    back[127] = inner(g[0], g[1])
    back[128] = inner(g[1], g[1])
    back[129] = inner(g[0], h)
    back[130] = inner(g[1], h)
    back[131] = jnp.zeros(TILE, F32)

    for j in range(1, 8):
        _, lane, ahead = picks(j)
        p = [near[(j - 1) * 6 + n] for n in range(6)]
        o = [forward(*p[0:3]), forward(*p[3:6])]
        mix = [[-inner(g[a], o[b]) for b in range(2)] for a in range(2)]
        for q in range(9):
            c0 = pick(q, j, lane, ahead)
            c1 = pick(9 + q, j, lane, ahead)
            for a in range(2):
                mixed[(j - 1) * 18 + a * 9 + q] = mix[a][0] * c0 + mix[a][1] * c1
    for k in range(RANKS):
        hits = [ranks[k] == j for j in range(1, 8)]
        for n in range(18):
            out = jnp.zeros(TILE, F32)
            for j in range(7):
                out = jnp.where(hits[j], mixed[j * 18 + n], out)
            back[k * 18 + n] = out
    for row in range(ROWS_BACK):
        tiles = [back[row * 4 + t] for t in range(4)]
        tiles = [pltpu.roll(tile, t * GROUP, 1) if t else tile for t, tile in enumerate(tiles)]
        for m in range(4):
            out = tiles[0]
            for t in range(1, 4):
                out = jnp.where(group == (t + m) % 4, tiles[t], out)
            msg[pl.ds(m * ROWS_BACK + row, 8, stride=4 * ROWS_BACK), :] = out


def build_right(turn, back, own, pair_slot, right_hi, right_lo, flat):
    group = lane_groups()
    low = lax.broadcasted_iota(jnp.int32, TILE, 0)
    for row in range(ROWS_BACK):
        ins = [back[pl.ds(m * ROWS_BACK + row, 8, stride=4 * ROWS_BACK), :] for m in range(4)]
        for t, tile in enumerate(regroup(ins, group)):
            at = row * 32 + ((t - turn) & 3) * 8
            flat[pl.ds(pl.multiple_of(at, 8), 8), :] = tile
    for d in range(CHUNKS):
        cols = slice(d * LANES, (d + 1) * LANES)

        def spread(u):
            return jnp.broadcast_to(flat[u * 8 + d : u * 8 + d + 1, :], TILE)

        def mine(u):
            return jnp.broadcast_to(own[u : u + 1, cols], TILE)

        cam = mine(26).astype(jnp.int32)
        m00, m01, m11 = spread(126), spread(127), spread(128)
        grad = [mine(24) - spread(129), mine(25) - spread(130)]
        total = {}
        for q in range(9):
            c0, c1 = mine(q), mine(9 + q)
            diag = [c0 - m00 * c0 - m01 * c1, c1 - m01 * c0 - m11 * c1]
            for i in range(2):
                tail = jnp.where(low == 6, diag[i], 0.0)
                if q == 0:
                    tail = jnp.where(low == 7, grad[i], tail)
                total[q, i, 1] = tail
        for k in range(RANKS):
            slot = jnp.broadcast_to(pair_slot[k : k + 1, cols], TILE)
            o = jnp.where(slot == CAM_ROW * 8 * NBR, -1, slot - cam * NBR)
            hits = [o == low, o == low + 8]
            for q in range(9):
                for i in range(2):
                    n = spread(k * 18 + i * 9 + q)
                    for side in range(2):
                        term = jnp.where(hits[side], n, 0.0)
                        total[q, i, side] = term if (q, i, side) not in total else total[q, i, side] + term
        wide = slice(d * 2 * LANES, (d + 1) * 2 * LANES)
        for q in range(9):
            for side in range(2):
                value = jnp.concatenate([total[q, 0, side], total[q, 1, side]], axis=1)
                hi = value.astype(BF16)
                at = slice(q * 16 + side * 8, q * 16 + side * 8 + 8)
                right_hi[at, wide] = hi
                right_lo[at, wide] = (value - hi.astype(F32)).astype(BF16)


def dot_t(x, y):
    return lax.dot_general(x, y, (((1,), (1,)), ((), ())), preferred_element_type=F32)


def build_blocks(dests, own, split, right_hi, right_lo, left, wide, outs):
    count = len(dests)
    low = lax.broadcasted_iota(jnp.int32, TILE, 0)
    bases = [(dest * CAM_ROW + low).astype(F32) for dest in dests]
    for d in range(CHUNKS):
        cols = slice(d * LANES, (d + 1) * LANES)
        cam = jnp.broadcast_to(own[26:27, cols], TILE)
        hits = [[cam == base, cam == base + 8.0] for base in bases]
        span = slice(d * 2 * LANES, (d + 1) * 2 * LANES)
        for p in range(9):
            for part in range(2):
                values = [jnp.broadcast_to(split[u : u + 1, cols], TILE) for u in (part * 24 + p, part * 24 + 9 + p)]
                for n in range(count):
                    for side in range(2):
                        at = (part * count + n) * SIDE + p * 16 + side * 8
                        both = [jnp.where(hits[n][side], value, 0.0) for value in values]
                        left[at : at + 8, span] = jnp.concatenate(both, axis=1).astype(BF16)
    size = count * SIDE
    by_hi = dot_t(left[0 : 2 * size, :], right_hi[...])
    by_lo = dot_t(left[0:size, :], right_lo[...])
    total = by_hi[0:size] + (by_hi[size : 2 * size] + by_lo)
    lane = lax.broadcasted_iota(jnp.int32, (16, LANES), 1)
    for n, out in enumerate(outs):
        block = total[n * SIDE : (n + 1) * SIDE]
        out[0:SIDE, :] = block[:, :LANES]
        wide[:, 0:16] = block[:, LANES:]
        tail = wide[0:16, :]
        for p in range(1, 8):
            tail = jnp.where(lane // 16 == p, pltpu.roll(wide[p * 16 : p * 16 + 16, :], p * 16, 1), tail)
        out[SIDE : SIDE + 16, :] = tail
        out[SIDE + 16 : BLOCK, :] = wide[128:144, :]


def first_kernel(back, own, split, pair_slot, block, right_hi, right_lo, left, wide, flat):
    build_right(lax.axis_index("obs") & 3, back, own, pair_slot, right_hi, right_lo, flat)
    wide[...] = jnp.zeros((SIDE, LANES), F32)
    build_blocks([(lax.axis_index("row") + 4) & 7], own, split, right_hi, right_lo, left, wide, [block])


def next_kernel(shifts, own, split, right_hi, right_lo, *rest):
    outs, (left, wide) = rest[: len(shifts)], rest[len(shifts) :]
    wide[...] = jnp.zeros((SIDE, LANES), F32)
    build_blocks([(lax.axis_index("row") + s) & 7 for s in shifts], own, split, right_hi, right_lo, left, wide, outs)


def final_kernel(own, plus1, minus1, plus2, minus2, hess, grad, pair, body, last, rows):
    body[...] = own[...] + ((plus1[...] + minus1[...]) + (plus2[...] + minus2[...]))
    for p in range(8):
        piece = body[SIDE : SIDE + 16, :]
        last[p * 16 : p * 16 + 16, :] = piece if p == 0 else pltpu.roll(piece, (LANES - p * 16) % LANES, 1)
    last[128:144, :] = body[SIDE + 16 : BLOCK, :]
    lane = lax.broadcasted_iota(jnp.int32, (9, LANES), 1)
    grads = jnp.zeros((9, LANES), F32)
    for q in range(9):
        halves = [jnp.zeros((9, LANES), F32), jnp.zeros((9, LANES), F32)]
        for c in range(CAM_ROW):
            ref, at = (body, q * 16) if q < 8 else (last, 0)
            x = ref[pl.ds(c, 9, stride=16), :]
            turn = pltpu.roll(x, (c * NBR - at) % LANES, 1)
            for half in range(2):
                lo, hi = c * NBR - half * LANES, (c + 1) * NBR - half * LANES
                if hi > 0 and lo < LANES:
                    halves[half] = jnp.where((lane >= lo) & (lane < hi), turn, halves[half])
            if q == 0:
                grads = jnp.where(lane == c, pltpu.roll(x, (c - at - 15) % LANES, 1), grads)
        for n, x in enumerate(halves):
            rows[pl.ds(n * 88 + q, 9, stride=9), :] = x
    pair[:, 0:LANES] = rows[0:81, :]
    pair[:, LANES : CAM_ROW * NBR] = rows[88:169, : CAM_ROW * NBR - LANES]
    lane = lax.broadcasted_iota(jnp.int32, TILE, 1)
    for half in range(2):
        diag = jnp.zeros(TILE, F32)
        for p in range(9):
            at = p * 16 + half * 8
            q = lane - p * 9
            x = jnp.take_along_axis(body[at : at + 8, :], (q * 16 + 14) & (LANES - 1), axis=1)
            diag = jnp.where((q >= 0) & (q < 8), x, diag)
            x = pltpu.roll(last[at : at + 8, :], (p * 9 + 8 - 14) % LANES, 1)
            diag = jnp.where(q == 8, x, diag)
        hess[half * 8 : half * 8 + 8, :] = diag[:, :81]
    grad[...] = grads[:, :CAM_ROW]


def on_device(
    camera_jacobian, point_jacobian, residual, send_order, camera_of, track_of, partner, pair_slot
):
    peers = lax.axis_size("obs")
    order = send_order.reshape(1, SLOTS)
    raw = (camera_jacobian, point_jacobian, residual, camera_of.reshape(1, SLOTS), order)
    msg = pl.pallas_call(
        pack_kernel,
        out_shape=jax.ShapeDtypeStruct((peers * ROWS_IN, LANES), F32),
        in_specs=[pl.BlockSpec(memory_space=pltpu.HBM)] * 5,
        scratch_shapes=[
            pltpu.VMEM((32, SLOTS), F32),
            pltpu.VMEM((18, SLOTS), F32),
            pltpu.VMEM((6, SLOTS), F32),
            pltpu.VMEM((2, SLOTS), F32),
            pltpu.VMEM((1, SLOTS), jnp.int32),
            pltpu.VMEM((1, SLOTS), jnp.int32),
            pltpu.SemaphoreType.DMA((5,)),
        ],
        compiler_params=PARAMS,
        name="pack",
    )(*[pltpu.with_memory_space_constraint(x, pltpu.HBM) for x in raw])
    owned = lax.all_to_all(msg.reshape(peers, ROWS_IN, LANES), "obs", 0, 0, tiled=True)
    returned = pl.pallas_call(
        owner_kernel,
        out_shape=jax.ShapeDtypeStruct((peers * ROWS_BACK, LANES), F32),
        scratch_shapes=[
            pltpu.VMEM((RANKS * 8, LANES), jnp.int32),
            pltpu.VMEM((8 * 52, 8, LANES), F32),
            pltpu.VMEM((RANKS * 6, 8, LANES), F32),
            pltpu.VMEM((RANKS * 18, 8, LANES), F32),
            pltpu.VMEM((132, 8, LANES), F32),
        ],
        compiler_params=PARAMS,
        name="owner",
    )(owned.reshape(peers * ROWS_IN, LANES), partner)
    back = lax.all_to_all(returned.reshape(peers, 1, ROWS_BACK * LANES), "obs", 0, 0, tiled=True)
    block = jax.ShapeDtypeStruct((BLOCK, LANES), F32)
    side = jax.ShapeDtypeStruct((SIDE, 2 * SLOTS), BF16)
    own, split = pl.pallas_call(
        own_kernel,
        out_shape=(jax.ShapeDtypeStruct((32, SLOTS), F32), jax.ShapeDtypeStruct((48, SLOTS), F32)),
        scratch_shapes=[pltpu.VMEM((32, SLOTS), F32)],
        compiler_params=PARAMS,
        cost_estimate=COST,
        name="own",
    )(*raw)

    def scratch(count):
        return [pltpu.VMEM((2 * count * SIDE, 2 * SLOTS), BF16), pltpu.VMEM((SIDE, LANES), F32)]

    far, right_hi, right_lo = pl.pallas_call(
        first_kernel,
        out_shape=(block, side, side),
        scratch_shapes=scratch(1) + [pltpu.VMEM((132 * 8, LANES), F32)],
        compiler_params=PARAMS,
        cost_estimate=COST,
        name="camera_0",
    )(back.reshape(peers * ROWS_BACK, LANES), own, split, pair_slot)

    def blocks(shifts):
        return pl.pallas_call(
            functools.partial(next_kernel, shifts),
                out_shape=(block,) * len(shifts),
            scratch_shapes=scratch(len(shifts)),
            compiler_params=PARAMS,
            cost_estimate=COST,
        )(own, split, right_hi, right_lo)

    def shift(x, by):
        return lax.ppermute(x, "row", [(n, (n + by) % 8) for n in range(8)])

    far = shift(far, 2)
    plus, minus = blocks((3, 5))
    plus, minus = shift(plus, 1), shift(minus, -1)
    plus2, minus2 = blocks((2, 6))
    plus1, minus1 = blocks((1, 7))
    plus2 = shift(plus2 + (plus + far), 2)
    minus2 = shift(minus2 + minus, -2)
    plus1, minus1 = shift(plus1, 1), shift(minus1, -1)
    (kept,) = blocks((0,))
    hess, grad, pair = pl.pallas_call(
        final_kernel,
        out_shape=(
            jax.ShapeDtypeStruct((CAM_ROW, 81), F32),
            jax.ShapeDtypeStruct((9, CAM_ROW), F32),
            jax.ShapeDtypeStruct((81, CAM_ROW * NBR), F32),
        ),
        scratch_shapes=[
            pltpu.VMEM((BLOCK, LANES), F32),
            pltpu.VMEM((SIDE, LANES), F32),
            pltpu.VMEM((176, LANES), F32),
        ],
        compiler_params=PARAMS,
        name="final",
    )(kept, plus1, minus1, plus2, minus2)
    return hess.T, grad, pair


def solution(mesh):
    return jax.shard_map(
        on_device,
        mesh=mesh,
        in_specs=(
            P(None, ("obs", "row")),
            P(None, ("obs", "row")),
            P(None, ("obs", "row")),
            P(("obs", "row")),
            P(("obs", "row")),
            P(("obs", "row")),
            P(None, ("obs", "row")),
            P(None, ("obs", "row")),
        ),
        out_specs=(P(None, ("obs", "row")), P(None, ("obs", "row")), P(None, ("obs", "row"))),
        check_vma=False,
    )
```

```python
import functools

import jax
import jax.numpy as jnp
from jax import lax
from jax.experimental import pallas as pl
from jax.experimental.pallas import tpu as pltpu
from jax.sharding import PartitionSpec as P


CAM_ROW = 16
NBR = 14
RANKS = 7
LANES = 128
GROUP = 32
SLOTS = 1024
CHUNKS = SLOTS // LANES
ROWS_IN = 8
ROWS_BACK = 33
SIDE = 144
BLOCK = 176
damping = 1.0
COST = pl.CostEstimate(flops=4_000_000_000, bytes_accessed=4_000_000, transcendentals=0)
PARAMS = pltpu.CompilerParams(vmem_limit_bytes=16 << 20)
F32 = jnp.float32
BF16 = jnp.bfloat16
TILE = (8, LANES)


def lane_groups():
    return lax.broadcasted_iota(jnp.int32, TILE, 1) // GROUP


def regroup(parts, group):
    outs = []
    for a in range(4):
        out = parts[a]
        for b in range(4):
            if b != a:
                out = jnp.where(group == b, pltpu.roll(parts[b], ((b - a) * GROUP) % LANES, 1), out)
        outs.append(out)
    return outs


def ordered(rows, order, d, t):
    idx = jnp.broadcast_to(order[0:1, d * LANES : (d + 1) * LANES], TILE)
    part = idx // LANES
    lane = idx % LANES
    out = None
    for s in range(CHUNKS):
        got = jnp.take_along_axis(rows[t * 8 : t * 8 + 8, s * LANES : (s + 1) * LANES], lane, axis=1)
        out = got if out is None else jnp.where(part == s, got, out)
    return out


def fill_rows(jc, jp, err, cam, rows):
    rows[0:18, :] = jc[...]
    rows[18:24, :] = jp[...]
    rows[24:26, :] = err[...]
    rows[26:27, :] = cam[...].astype(F32)
    rows[27:32, :] = jnp.zeros((5, SLOTS), F32)


def pack_kernel(*refs):
    sources, (msg, own, split, rows, *targets, sems) = refs[:5], refs[5:]
    copies = [pltpu.make_async_copy(x, y, sems.at[n]) for n, (x, y) in enumerate(zip(sources, targets))]
    for copy in copies:
        copy.start()
    for copy in copies:
        copy.wait()
    jc, jp, err, cam, order = targets
    fill_rows(jc, jp, err, cam, rows)
    group = lane_groups()
    for d in range(CHUNKS):
        cols = slice(d * LANES, (d + 1) * LANES)
        tiles = [ordered(rows, order, d, t) for t in range(4)]
        for t, value in enumerate(tiles):
            own[t * 8 : t * 8 + 8, cols] = value
            if t < 3:
                hi = value.astype(BF16).astype(F32)
                split[t * 8 : t * 8 + 8, cols] = hi
                split[24 + t * 8 : 32 + t * 8, cols] = (value - hi).astype(BF16).astype(F32)
        for m, tile in enumerate(regroup(tiles, group)):
            msg[(d * 4 + m) * ROWS_IN : (d * 4 + m) * ROWS_IN + 8, :] = tile


def owner_kernel(owned, partner, msg, slots, turned, near, mixed, back, plan):
    group = lane_groups()
    for r in range(8):
        slots[pl.ds(r, RANKS, stride=8), :] = partner[:, r * LANES : (r + 1) * LANES]
    for row in range(ROWS_IN):
        ins = [owned[pl.ds(m * ROWS_IN + row, 8, stride=4 * ROWS_IN), :] for m in range(4)]
        for t, tile in enumerate(regroup(ins, group)):
            u = t * 8 + row
            if u >= 26:
                continue
            turned[u] = tile
            for b in range(4):
                lanes = pltpu.roll(tile, LANES - b * GROUP, 1) if b else tile
                up = [lanes, pltpu.roll(lanes, 7, 0), pltpu.roll(lanes, 6, 0)] if b else [lanes, pltpu.roll(lanes, 7, 0)]
                for a in range(2):
                    j = a * 4 + b
                    if j:
                        here = jnp.where(group < 4 - b, up[a], up[a + 1]) if b else up[a]
                        turned[j * 52 + u] = here
                        turned[j * 52 + 26 + u] = pltpu.roll(here, 2, 0)
    source = lax.broadcasted_iota(jnp.int32, TILE, 0) * 4 + group
    ranks, words = [], []
    for k in range(RANKS):
        idx = slots[k * 8 : k * 8 + 8, :]
        apart = (idx // GROUP - source) & 31
        ranks.append(apart & 7)
        words.append((idx & 31) + jnp.where(apart < 16, GROUP, 0))
        plan[k] = ranks[k]
    for j in range(1, 8):
        word = jnp.full(TILE, -1, jnp.int32)
        for k in range(RANKS):
            word = jnp.where(ranks[k] == j, words[k], word)
        plan[6 + j] = word

    def picks(j):
        word = plan[6 + j]
        return word >= 0, group * GROUP + (word & 31), word >= GROUP

    def pick(u, j, lane, ahead):
        front = jnp.take_along_axis(turned[j * 52 + u], lane, axis=1)
        behind = jnp.take_along_axis(turned[j * 52 + 26 + u], lane, axis=1)
        return jnp.where(ahead, front, behind)

    def normal(p, e):
        out = []
        for a in range(3):
            for b in range(a, 3):
                out.append(p[a] * p[b] + p[3 + a] * p[3 + b])
        for a in range(3):
            out.append(p[a] * e[0] + p[3 + a] * e[1])
        return out

    mine = [turned[18 + n] for n in range(8)]
    total = normal(mine[:6], mine[6:])
    for j in range(1, 8):
        valid, lane, ahead = picks(j)
        got = [jnp.where(valid, pick(18 + n, j, lane, ahead), 0.0) for n in range(8)]
        for n in range(6):
            near[(j - 1) * 6 + n] = got[n]
        total = [x + y for x, y in zip(total, normal(got[:6], got[6:]))]
    v00, v01, v02, v11, v12, v22, b0, b1, b2 = total
    i0 = 1.0 / jnp.sqrt(v00 + damping)
    l10 = v01 * i0
    l20 = v02 * i0
    i1 = 1.0 / jnp.sqrt(v11 + damping - l10 * l10)
    l21 = (v12 - l20 * l10) * i1
    i2 = 1.0 / jnp.sqrt(v22 + damping - l20 * l20 - l21 * l21)

    def forward(x0, x1, x2):
        y0 = x0 * i0
        y1 = (x1 - l10 * y0) * i1
        y2 = (x2 - l20 * y0 - l21 * y1) * i2
        return y0, y1, y2

    def inner(x, y):
        return x[0] * y[0] + x[1] * y[1] + x[2] * y[2]

    h = forward(b0, b1, b2)
    g = [forward(*mine[0:3]), forward(*mine[3:6])]
    back[0] = inner(g[0], g[0])
    back[1] = inner(g[0], g[1])
    back[2] = inner(g[1], g[1])
    back[3] = inner(g[0], h)
    back[4] = inner(g[1], h)
    back[5] = jnp.zeros(TILE, F32)

    for j in range(1, 8):
        _, lane, ahead = picks(j)
        p = [near[(j - 1) * 6 + n] for n in range(6)]
        o = [forward(*p[0:3]), forward(*p[3:6])]
        mix = [[-inner(g[a], o[b]) for b in range(2)] for a in range(2)]
        for q in range(9):
            c0 = pick(q, j, lane, ahead)
            c1 = pick(9 + q, j, lane, ahead)
            for a in range(2):
                mixed[(j - 1) * 18 + a * 9 + q] = mix[a][0] * c0 + mix[a][1] * c1

    def ranked(u):
        k, n = divmod(u, 18)
        if k >= RANKS:
            return back[n]
        rank = plan[k]
        out = jnp.zeros(TILE, F32)
        for j in range(7):
            out = jnp.where(rank == j + 1, mixed[j * 18 + n], out)
        return out

    for row in range(ROWS_BACK):
        tiles = [ranked(row * 4 + t) for t in range(4)]
        tiles = [pltpu.roll(tile, t * GROUP, 1) if t else tile for t, tile in enumerate(tiles)]
        for m in range(4):
            out = tiles[0]
            for t in range(1, 4):
                out = jnp.where(group == (t + m) % 4, tiles[t], out)
            msg[pl.ds(m * ROWS_BACK + row, 8, stride=4 * ROWS_BACK), :] = out


def build_right(turn, back, own, pair_slot, right_hi, right_lo, flat):
    group = lane_groups()
    low = lax.broadcasted_iota(jnp.int32, TILE, 0)
    for row in range(ROWS_BACK):
        ins = [back[pl.ds(m * ROWS_BACK + row, 8, stride=4 * ROWS_BACK), :] for m in range(4)]
        for t, tile in enumerate(regroup(ins, group)):
            at = row * 32 + ((t - turn) & 3) * 8
            flat[pl.ds(pl.multiple_of(at, 8), 8), :] = tile
    for d in range(CHUNKS):
        cols = slice(d * LANES, (d + 1) * LANES)

        def spread(u):
            return jnp.broadcast_to(flat[u * 8 + d : u * 8 + d + 1, :], TILE)

        def mine(u):
            return jnp.broadcast_to(own[u : u + 1, cols], TILE)

        cam = mine(26).astype(jnp.int32)
        m00, m01, m11 = spread(126), spread(127), spread(128)
        grad = [mine(24) - spread(129), mine(25) - spread(130)]
        total = {}
        for q in range(9):
            c0, c1 = mine(q), mine(9 + q)
            diag = [c0 - m00 * c0 - m01 * c1, c1 - m01 * c0 - m11 * c1]
            for i in range(2):
                tail = jnp.where(low == 6, diag[i], 0.0)
                if q == 0:
                    tail = jnp.where(low == 7, grad[i], tail)
                total[q, i, 1] = tail
        for k in range(RANKS):
            slot = jnp.broadcast_to(pair_slot[k : k + 1, cols], TILE)
            o = jnp.where(slot == CAM_ROW * 8 * NBR, -1, slot - cam * NBR)
            hits = [o == low, o == low + 8]
            for q in range(9):
                for i in range(2):
                    n = spread(k * 18 + i * 9 + q)
                    for side in range(2):
                        term = jnp.where(hits[side], n, 0.0)
                        total[q, i, side] = term if (q, i, side) not in total else total[q, i, side] + term
        wide = slice(d * 2 * LANES, (d + 1) * 2 * LANES)
        for q in range(9):
            for side in range(2):
                value = jnp.concatenate([total[q, 0, side], total[q, 1, side]], axis=1)
                hi = value.astype(BF16)
                at = slice(q * 16 + side * 8, q * 16 + side * 8 + 8)
                right_hi[at, wide] = hi
                right_lo[at, wide] = (value - hi.astype(F32)).astype(BF16)


def dot_t(x, y):
    return lax.dot_general(x, y, (((1,), (1,)), ((), ())), preferred_element_type=F32)


def build_blocks(dests, own, split, right_hi, right_lo, left, wide, outs):
    count = len(dests)
    low = lax.broadcasted_iota(jnp.int32, TILE, 0)
    bases = [(dest * CAM_ROW + low).astype(F32) for dest in dests]
    for d in range(CHUNKS):
        cols = slice(d * LANES, (d + 1) * LANES)
        cam = jnp.broadcast_to(own[26:27, cols], TILE)
        hits = [[cam == base, cam == base + 8.0] for base in bases]
        span = slice(d * 2 * LANES, (d + 1) * 2 * LANES)
        for p in range(9):
            for part in range(2):
                values = [jnp.broadcast_to(split[u : u + 1, cols], TILE) for u in (part * 24 + p, part * 24 + 9 + p)]
                for n in range(count):
                    for side in range(2):
                        at = (part * count + n) * SIDE + p * 16 + side * 8
                        both = [jnp.where(hits[n][side], value, 0.0) for value in values]
                        left[at : at + 8, span] = jnp.concatenate(both, axis=1).astype(BF16)
    size = count * SIDE
    by_hi = dot_t(left[0 : 2 * size, :], right_hi[...])
    by_lo = dot_t(left[0:size, :], right_lo[...])
    total = by_hi[0:size] + (by_hi[size : 2 * size] + by_lo)
    lane = lax.broadcasted_iota(jnp.int32, (16, LANES), 1)
    for n, out in enumerate(outs):
        block = total[n * SIDE : (n + 1) * SIDE]
        out[0:SIDE, :] = block[:, :LANES]
        wide[:, 0:16] = block[:, LANES:]
        tail = wide[0:16, :]
        for p in range(1, 8):
            tail = jnp.where(lane // 16 == p, pltpu.roll(wide[p * 16 : p * 16 + 16, :], p * 16, 1), tail)
        out[SIDE : SIDE + 16, :] = tail
        out[SIDE + 16 : BLOCK, :] = wide[128:144, :]


def first_kernel(back, own, split, pair_slot, block, right_hi, right_lo, left, wide, flat):
    build_right(lax.axis_index("obs") & 3, back, own, pair_slot, right_hi, right_lo, flat)
    wide[...] = jnp.zeros((SIDE, LANES), F32)
    build_blocks([(lax.axis_index("row") + 4) & 7], own, split, right_hi, right_lo, left, wide, [block])


def next_kernel(shifts, own, split, right_hi, right_lo, *rest):
    outs, (left, wide) = rest[: len(shifts)], rest[len(shifts) :]
    wide[...] = jnp.zeros((SIDE, LANES), F32)
    build_blocks([(lax.axis_index("row") + s) & 7 for s in shifts], own, split, right_hi, right_lo, left, wide, outs)


def final_kernel(own, plus1, minus1, plus2, minus2, hess, grad, pair, body, last, rows):
    body[...] = own[...] + ((plus1[...] + minus1[...]) + (plus2[...] + minus2[...]))
    for p in range(8):
        piece = body[SIDE : SIDE + 16, :]
        last[p * 16 : p * 16 + 16, :] = piece if p == 0 else pltpu.roll(piece, (LANES - p * 16) % LANES, 1)
    last[128:144, :] = body[SIDE + 16 : BLOCK, :]
    lane = lax.broadcasted_iota(jnp.int32, (9, LANES), 1)
    grads = jnp.zeros((9, LANES), F32)
    for q in range(9):
        halves = [jnp.zeros((9, LANES), F32), jnp.zeros((9, LANES), F32)]
        for c in range(CAM_ROW):
            ref, at = (body, q * 16) if q < 8 else (last, 0)
            x = ref[pl.ds(c, 9, stride=16), :]
            turn = pltpu.roll(x, (c * NBR - at) % LANES, 1)
            for half in range(2):
                lo, hi = c * NBR - half * LANES, (c + 1) * NBR - half * LANES
                if hi > 0 and lo < LANES:
                    halves[half] = jnp.where((lane >= lo) & (lane < hi), turn, halves[half])
            if q == 0:
                grads = jnp.where(lane == c, pltpu.roll(x, (c - at - 15) % LANES, 1), grads)
        for n, x in enumerate(halves):
            rows[pl.ds(n * 88 + q, 9, stride=9), :] = x
    pair[:, 0:LANES] = rows[0:81, :]
    pair[:, LANES : CAM_ROW * NBR] = rows[88:169, : CAM_ROW * NBR - LANES]
    lane = lax.broadcasted_iota(jnp.int32, TILE, 1)
    for half in range(2):
        diag = jnp.zeros(TILE, F32)
        for p in range(9):
            at = p * 16 + half * 8
            q = lane - p * 9
            x = jnp.take_along_axis(body[at : at + 8, :], (q * 16 + 14) & (LANES - 1), axis=1)
            diag = jnp.where((q >= 0) & (q < 8), x, diag)
            x = pltpu.roll(last[at : at + 8, :], (p * 9 + 8 - 14) % LANES, 1)
            diag = jnp.where(q == 8, x, diag)
        hess[half * 8 : half * 8 + 8, :] = diag[:, :81]
    grad[...] = grads[:, :CAM_ROW]


def on_device(
    camera_jacobian, point_jacobian, residual, send_order, camera_of, track_of, partner, pair_slot
):
    peers = lax.axis_size("obs")
    order = send_order.reshape(1, SLOTS)
    raw = (camera_jacobian, point_jacobian, residual, camera_of.reshape(1, SLOTS), order)
    msg, own, split = pl.pallas_call(
        pack_kernel,
        out_shape=(
            jax.ShapeDtypeStruct((peers * ROWS_IN, LANES), F32),
            jax.ShapeDtypeStruct((32, SLOTS), F32),
            jax.ShapeDtypeStruct((48, SLOTS), F32),
        ),
        in_specs=[pl.BlockSpec(memory_space=pltpu.HBM)] * 5,
        scratch_shapes=[
            pltpu.VMEM((32, SLOTS), F32),
            pltpu.VMEM((18, SLOTS), F32),
            pltpu.VMEM((6, SLOTS), F32),
            pltpu.VMEM((2, SLOTS), F32),
            pltpu.VMEM((1, SLOTS), jnp.int32),
            pltpu.VMEM((1, SLOTS), jnp.int32),
            pltpu.SemaphoreType.DMA((5,)),
        ],
        compiler_params=PARAMS,
        name="pack",
    )(*[pltpu.with_memory_space_constraint(x, pltpu.HBM) for x in raw])
    owned = lax.all_to_all(msg.reshape(peers, ROWS_IN, LANES), "obs", 0, 0, tiled=True)
    returned = pl.pallas_call(
        owner_kernel,
        out_shape=jax.ShapeDtypeStruct((peers * ROWS_BACK, LANES), F32),
        scratch_shapes=[
            pltpu.VMEM((RANKS * 8, LANES), jnp.int32),
            pltpu.VMEM((8 * 52, 8, LANES), F32),
            pltpu.VMEM((RANKS * 6, 8, LANES), F32),
            pltpu.VMEM((RANKS * 18, 8, LANES), F32),
            pltpu.VMEM((6, 8, LANES), F32),
            pltpu.VMEM((14, 8, LANES), jnp.int32),
        ],
        compiler_params=PARAMS,
        name="owner",
    )(owned.reshape(peers * ROWS_IN, LANES), partner)
    back = lax.all_to_all(returned.reshape(peers, 1, ROWS_BACK * LANES), "obs", 0, 0, tiled=True)
    block = jax.ShapeDtypeStruct((BLOCK, LANES), F32)
    side = jax.ShapeDtypeStruct((SIDE, 2 * SLOTS), BF16)

    def scratch(count):
        return [pltpu.VMEM((2 * count * SIDE, 2 * SLOTS), BF16), pltpu.VMEM((SIDE, LANES), F32)]

    far, right_hi, right_lo = pl.pallas_call(
        first_kernel,
        out_shape=(block, side, side),
        scratch_shapes=scratch(1) + [pltpu.VMEM((132 * 8, LANES), F32)],
        compiler_params=PARAMS,
        cost_estimate=COST,
        name="camera_0",
    )(back.reshape(peers * ROWS_BACK, LANES), own, split, pair_slot)

    def blocks(shifts):
        return pl.pallas_call(
            functools.partial(next_kernel, shifts),
                out_shape=(block,) * len(shifts),
            scratch_shapes=scratch(len(shifts)),
            compiler_params=PARAMS,
            cost_estimate=COST,
        )(own, split, right_hi, right_lo)

    def shift(x, by):
        return lax.ppermute(x, "row", [(n, (n + by) % 8) for n in range(8)])

    far = shift(far, 2)
    plus, minus = blocks((3, 5))
    plus, minus = shift(plus, 1), shift(minus, -1)
    plus2, minus2 = blocks((2, 6))
    plus1, minus1 = blocks((1, 7))
    plus2 = shift(plus2 + (plus + far), 2)
    minus2 = shift(minus2 + minus, -2)
    plus1, minus1 = shift(plus1, 1), shift(minus1, -1)
    (kept,) = blocks((0,))
    hess, grad, pair = pl.pallas_call(
        final_kernel,
        out_shape=(
            jax.ShapeDtypeStruct((CAM_ROW, 81), F32),
            jax.ShapeDtypeStruct((9, CAM_ROW), F32),
            jax.ShapeDtypeStruct((81, CAM_ROW * NBR), F32),
        ),
        scratch_shapes=[
            pltpu.VMEM((BLOCK, LANES), F32),
            pltpu.VMEM((SIDE, LANES), F32),
            pltpu.VMEM((176, LANES), F32),
        ],
        compiler_params=PARAMS,
        name="final",
    )(kept, plus1, minus1, plus2, minus2)
    return hess.T, grad, pair


def solution(mesh):
    return jax.shard_map(
        on_device,
        mesh=mesh,
        in_specs=(
            P(None, ("obs", "row")),
            P(None, ("obs", "row")),
            P(None, ("obs", "row")),
            P(("obs", "row")),
            P(("obs", "row")),
            P(("obs", "row")),
            P(None, ("obs", "row")),
            P(None, ("obs", "row")),
        ),
        out_specs=(P(None, ("obs", "row")), P(None, ("obs", "row")), P(None, ("obs", "row"))),
        check_vma=False,
    )
```

```python
import functools

import jax
import jax.numpy as jnp
from jax import lax
from jax.experimental import pallas as pl
from jax.experimental.pallas import tpu as pltpu
from jax.sharding import PartitionSpec as P


CAM_ROW = 16
NBR = 14
RANKS = 7
LANES = 128
GROUP = 32
SLOTS = 1024
CHUNKS = SLOTS // LANES
ROWS_IN = 8
ROWS_BACK = 33
SIDE = 144
BLOCK = 168
damping = 1.0
COST = pl.CostEstimate(flops=4_000_000_000, bytes_accessed=4_000_000, transcendentals=0)
PARAMS = pltpu.CompilerParams(vmem_limit_bytes=16 << 20)
F32 = jnp.float32
BF16 = jnp.bfloat16
TILE = (8, LANES)


def lane_groups():
    return lax.broadcasted_iota(jnp.int32, TILE, 1) // GROUP


def regroup(parts, group):
    outs = []
    for a in range(4):
        out = parts[a]
        for b in range(4):
            if b != a:
                out = jnp.where(group == b, pltpu.roll(parts[b], ((b - a) * GROUP) % LANES, 1), out)
        outs.append(out)
    return outs


def ordered(rows, order, d, t):
    idx = jnp.broadcast_to(order[0:1, d * LANES : (d + 1) * LANES], TILE)
    part = idx // LANES
    lane = idx % LANES
    out = None
    for s in range(CHUNKS):
        got = jnp.take_along_axis(rows[t * 8 : t * 8 + 8, s * LANES : (s + 1) * LANES], lane, axis=1)
        out = got if out is None else jnp.where(part == s, got, out)
    return out


def fill_rows(jc, jp, err, cam, rows):
    rows[0:18, :] = jc[...]
    rows[18:24, :] = jp[...]
    rows[24:26, :] = err[...]
    rows[26:27, :] = cam[...].astype(F32)
    rows[27:32, :] = jnp.zeros((5, SLOTS), F32)


def pack_kernel(*refs):
    sources, (msg, own, split, rows, *targets, sems) = refs[:5], refs[5:]
    copies = [pltpu.make_async_copy(x, y, sems.at[n]) for n, (x, y) in enumerate(zip(sources, targets))]
    for copy in copies:
        copy.start()
    for copy in copies:
        copy.wait()
    jc, jp, err, cam, order = targets
    fill_rows(jc, jp, err, cam, rows)
    group = lane_groups()
    for d in range(CHUNKS):
        cols = slice(d * LANES, (d + 1) * LANES)
        tiles = [ordered(rows, order, d, t) for t in range(4)]
        for t, value in enumerate(tiles):
            own[t * 8 : t * 8 + 8, cols] = value
            if t < 3:
                hi = value.astype(BF16).astype(F32)
                split[t * 8 : t * 8 + 8, cols] = hi
                split[24 + t * 8 : 32 + t * 8, cols] = (value - hi).astype(BF16).astype(F32)
        for m, tile in enumerate(regroup(tiles, group)):
            msg[(d * 4 + m) * ROWS_IN : (d * 4 + m) * ROWS_IN + 8, :] = tile


def owner_kernel(owned, partner, msg, slots, turned, near, mixed, back, plan):
    group = lane_groups()
    for r in range(8):
        slots[pl.ds(r, RANKS, stride=8), :] = partner[:, r * LANES : (r + 1) * LANES]
    for row in range(ROWS_IN):
        ins = [owned[pl.ds(m * ROWS_IN + row, 8, stride=4 * ROWS_IN), :] for m in range(4)]
        for t, tile in enumerate(regroup(ins, group)):
            u = t * 8 + row
            if u >= 26:
                continue
            turned[u] = tile
            for b in range(4):
                lanes = pltpu.roll(tile, LANES - b * GROUP, 1) if b else tile
                up = [lanes, pltpu.roll(lanes, 7, 0), pltpu.roll(lanes, 6, 0)] if b else [lanes, pltpu.roll(lanes, 7, 0)]
                for a in range(2):
                    j = a * 4 + b
                    if j:
                        here = jnp.where(group < 4 - b, up[a], up[a + 1]) if b else up[a]
                        turned[j * 52 + u] = here
                        turned[j * 52 + 26 + u] = pltpu.roll(here, 2, 0)
    source = lax.broadcasted_iota(jnp.int32, TILE, 0) * 4 + group
    ranks, words = [], []
    for k in range(RANKS):
        idx = slots[k * 8 : k * 8 + 8, :]
        apart = (idx // GROUP - source) & 31
        ranks.append(apart & 7)
        words.append((idx & 31) + jnp.where(apart < 16, GROUP, 0))
        plan[k] = ranks[k]
    for j in range(1, 8):
        word = jnp.full(TILE, -1, jnp.int32)
        for k in range(RANKS):
            word = jnp.where(ranks[k] == j, words[k], word)
        plan[6 + j] = word

    def picks(j):
        word = plan[6 + j]
        return word >= 0, group * GROUP + (word & 31), word >= GROUP

    def pick(u, j, lane, ahead):
        front = jnp.take_along_axis(turned[j * 52 + u], lane, axis=1)
        behind = jnp.take_along_axis(turned[j * 52 + 26 + u], lane, axis=1)
        return jnp.where(ahead, front, behind)

    def normal(p, e):
        out = []
        for a in range(3):
            for b in range(a, 3):
                out.append(p[a] * p[b] + p[3 + a] * p[3 + b])
        for a in range(3):
            out.append(p[a] * e[0] + p[3 + a] * e[1])
        return out

    mine = [turned[18 + n] for n in range(8)]
    total = normal(mine[:6], mine[6:])
    for j in range(1, 8):
        valid, lane, ahead = picks(j)
        got = [jnp.where(valid, pick(18 + n, j, lane, ahead), 0.0) for n in range(8)]
        for n in range(6):
            near[(j - 1) * 6 + n] = got[n]
        total = [x + y for x, y in zip(total, normal(got[:6], got[6:]))]
    v00, v01, v02, v11, v12, v22, b0, b1, b2 = total
    i0 = 1.0 / jnp.sqrt(v00 + damping)
    l10 = v01 * i0
    l20 = v02 * i0
    i1 = 1.0 / jnp.sqrt(v11 + damping - l10 * l10)
    l21 = (v12 - l20 * l10) * i1
    i2 = 1.0 / jnp.sqrt(v22 + damping - l20 * l20 - l21 * l21)

    def forward(x0, x1, x2):
        y0 = x0 * i0
        y1 = (x1 - l10 * y0) * i1
        y2 = (x2 - l20 * y0 - l21 * y1) * i2
        return y0, y1, y2

    def inner(x, y):
        return x[0] * y[0] + x[1] * y[1] + x[2] * y[2]

    h = forward(b0, b1, b2)
    g = [forward(*mine[0:3]), forward(*mine[3:6])]
    back[0] = inner(g[0], g[0])
    back[1] = inner(g[0], g[1])
    back[2] = inner(g[1], g[1])
    back[3] = inner(g[0], h)
    back[4] = inner(g[1], h)
    back[5] = jnp.zeros(TILE, F32)

    for j in range(1, 8):
        _, lane, ahead = picks(j)
        p = [near[(j - 1) * 6 + n] for n in range(6)]
        o = [forward(*p[0:3]), forward(*p[3:6])]
        mix = [[-inner(g[a], o[b]) for b in range(2)] for a in range(2)]
        for q in range(9):
            c0 = pick(q, j, lane, ahead)
            c1 = pick(9 + q, j, lane, ahead)
            for a in range(2):
                mixed[(j - 1) * 18 + a * 9 + q] = mix[a][0] * c0 + mix[a][1] * c1

    def ranked(u):
        k, n = divmod(u, 18)
        if k >= RANKS:
            return back[n]
        rank = plan[k]
        out = jnp.zeros(TILE, F32)
        for j in range(7):
            out = jnp.where(rank == j + 1, mixed[j * 18 + n], out)
        return out

    for row in range(ROWS_BACK):
        tiles = [ranked(row * 4 + t) for t in range(4)]
        tiles = [pltpu.roll(tile, t * GROUP, 1) if t else tile for t, tile in enumerate(tiles)]
        for m in range(4):
            out = tiles[0]
            for t in range(1, 4):
                out = jnp.where(group == (t + m) % 4, tiles[t], out)
            msg[pl.ds(m * ROWS_BACK + row, 8, stride=4 * ROWS_BACK), :] = out


def build_right(turn, back, own, pair_slot, right_hi, right_lo, flat):
    group = lane_groups()
    low = lax.broadcasted_iota(jnp.int32, TILE, 0)
    for row in range(ROWS_BACK):
        ins = [back[pl.ds(m * ROWS_BACK + row, 8, stride=4 * ROWS_BACK), :] for m in range(4)]
        for t, tile in enumerate(regroup(ins, group)):
            at = row * 32 + ((t - turn) & 3) * 8
            flat[pl.ds(pl.multiple_of(at, 8), 8), :] = tile
    for d in range(CHUNKS):
        cols = slice(d * LANES, (d + 1) * LANES)

        def spread(u):
            return jnp.broadcast_to(flat[u * 8 + d : u * 8 + d + 1, :], TILE)

        def mine(u):
            return jnp.broadcast_to(own[u : u + 1, cols], TILE)

        cam = mine(26).astype(jnp.int32)
        m00, m01, m11 = spread(126), spread(127), spread(128)
        grad = [mine(24) - spread(129), mine(25) - spread(130)]
        total = {}
        for q in range(9):
            c0, c1 = mine(q), mine(9 + q)
            diag = [c0 - m00 * c0 - m01 * c1, c1 - m01 * c0 - m11 * c1]
            for i in range(2):
                tail = jnp.where(low == 6, diag[i], 0.0)
                if q == 0:
                    tail = jnp.where(low == 7, grad[i], tail)
                total[q, i, 1] = tail
        for k in range(RANKS):
            slot = jnp.broadcast_to(pair_slot[k : k + 1, cols], TILE)
            o = jnp.where(slot == CAM_ROW * 8 * NBR, -1, slot - cam * NBR)
            hits = [o == low, o == low + 8]
            for q in range(9):
                for i in range(2):
                    n = spread(k * 18 + i * 9 + q)
                    for side in range(2):
                        term = jnp.where(hits[side], n, 0.0)
                        total[q, i, side] = term if (q, i, side) not in total else total[q, i, side] + term
        wide = slice(d * 2 * LANES, (d + 1) * 2 * LANES)
        for q in range(9):
            for side in range(2):
                value = jnp.concatenate([total[q, 0, side], total[q, 1, side]], axis=1)
                hi = value.astype(BF16)
                at = slice(q * 16 + side * 8, q * 16 + side * 8 + 8)
                right_hi[at, wide] = hi
                right_lo[at, wide] = (value - hi.astype(F32)).astype(BF16)


def dot_t(x, y):
    return lax.dot_general(x, y, (((1,), (1,)), ((), ())), preferred_element_type=F32)


def build_blocks(dests, own, split, right_hi, right_lo, left, wide, outs):
    count = len(dests)
    low = lax.broadcasted_iota(jnp.int32, TILE, 0)
    bases = [(dest * CAM_ROW + low).astype(F32) for dest in dests]
    for d in range(CHUNKS):
        cols = slice(d * LANES, (d + 1) * LANES)
        cam = jnp.broadcast_to(own[26:27, cols], TILE)
        hits = [[cam == base, cam == base + 8.0] for base in bases]
        span = slice(d * 2 * LANES, (d + 1) * 2 * LANES)
        for p in range(9):
            for part in range(2):
                values = [jnp.broadcast_to(split[u : u + 1, cols], TILE) for u in (part * 24 + p, part * 24 + 9 + p)]
                for n in range(count):
                    for side in range(2):
                        at = (part * count + n) * SIDE + p * 16 + side * 8
                        both = [jnp.where(hits[n][side], value, 0.0) for value in values]
                        left[at : at + 8, span] = jnp.concatenate(both, axis=1).astype(BF16)
    size = count * SIDE
    by_hi = dot_t(left[0 : 2 * size, :], right_hi[...])
    by_lo = dot_t(left[0:size, :], right_lo[...])
    total = by_hi[0:size] + (by_hi[size : 2 * size] + by_lo)
    lane = lax.broadcasted_iota(jnp.int32, (16, LANES), 1)
    for n, out in enumerate(outs):
        block = total[n * SIDE : (n + 1) * SIDE]
        out[0:SIDE, :] = block[:, :LANES]
        wide[:, 0:16] = block[:, LANES:]
        tail = wide[0:16, :]
        for p in range(1, 8):
            tail = jnp.where(lane // 16 == p, pltpu.roll(wide[p * 16 : p * 16 + 16, :], p * 16, 1), tail)
        out[SIDE : SIDE + 16, :] = tail
        out[SIDE + 16 : BLOCK, :] = jnp.where(lane[:8] // 16 == 1, pltpu.roll(wide[136:144, :], 16, 1), wide[128:136, :])


def first_kernel(back, own, split, pair_slot, block, right_hi, right_lo, left, wide, flat):
    build_right(lax.axis_index("obs") & 3, back, own, pair_slot, right_hi, right_lo, flat)
    wide[...] = jnp.zeros((SIDE, LANES), F32)
    build_blocks([(lax.axis_index("row") + 4) & 7], own, split, right_hi, right_lo, left, wide, [block])


def next_kernel(shifts, own, split, right_hi, right_lo, *rest):
    outs, (left, wide) = rest[: len(shifts)], rest[len(shifts) :]
    wide[...] = jnp.zeros((SIDE, LANES), F32)
    build_blocks([(lax.axis_index("row") + s) & 7 for s in shifts], own, split, right_hi, right_lo, left, wide, outs)


def final_kernel(own, plus1, minus1, plus2, minus2, hess, grad, pair, body, last, rows):
    body[...] = own[...] + ((plus1[...] + minus1[...]) + (plus2[...] + minus2[...]))
    for p in range(8):
        piece = body[SIDE : SIDE + 16, :]
        last[p * 16 : p * 16 + 16, :] = piece if p == 0 else pltpu.roll(piece, (LANES - p * 16) % LANES, 1)
    last[128:136, :] = body[SIDE + 16 : BLOCK, :]
    last[136:144, :] = pltpu.roll(body[SIDE + 16 : BLOCK, :], LANES - 16, 1)
    lane = lax.broadcasted_iota(jnp.int32, (9, LANES), 1)
    grads = jnp.zeros((9, LANES), F32)
    for q in range(9):
        halves = [jnp.zeros((9, LANES), F32), jnp.zeros((9, LANES), F32)]
        for c in range(CAM_ROW):
            ref, at = (body, q * 16) if q < 8 else (last, 0)
            x = ref[pl.ds(c, 9, stride=16), :]
            turn = pltpu.roll(x, (c * NBR - at) % LANES, 1)
            for half in range(2):
                lo, hi = c * NBR - half * LANES, (c + 1) * NBR - half * LANES
                if hi > 0 and lo < LANES:
                    halves[half] = jnp.where((lane >= lo) & (lane < hi), turn, halves[half])
            if q == 0:
                grads = jnp.where(lane == c, pltpu.roll(x, (c - at - 15) % LANES, 1), grads)
        for n, x in enumerate(halves):
            rows[pl.ds(n * 88 + q, 9, stride=9), :] = x
    pair[:, 0:LANES] = rows[0:81, :]
    pair[:, LANES : CAM_ROW * NBR] = rows[88:169, : CAM_ROW * NBR - LANES]
    lane = lax.broadcasted_iota(jnp.int32, TILE, 1)
    for half in range(2):
        diag = jnp.zeros(TILE, F32)
        for p in range(9):
            at = p * 16 + half * 8
            q = lane - p * 9
            x = jnp.take_along_axis(body[at : at + 8, :], (q * 16 + 14) & (LANES - 1), axis=1)
            diag = jnp.where((q >= 0) & (q < 8), x, diag)
            x = pltpu.roll(last[at : at + 8, :], (p * 9 + 8 - 14) % LANES, 1)
            diag = jnp.where(q == 8, x, diag)
        hess[half * 8 : half * 8 + 8, :] = diag[:, :81]
    grad[...] = grads[:, :CAM_ROW]


def on_device(
    camera_jacobian, point_jacobian, residual, send_order, camera_of, track_of, partner, pair_slot
):
    peers = lax.axis_size("obs")
    order = send_order.reshape(1, SLOTS)
    raw = (camera_jacobian, point_jacobian, residual, camera_of.reshape(1, SLOTS), order)
    msg, own, split = pl.pallas_call(
        pack_kernel,
        out_shape=(
            jax.ShapeDtypeStruct((peers * ROWS_IN, LANES), F32),
            jax.ShapeDtypeStruct((32, SLOTS), F32),
            jax.ShapeDtypeStruct((48, SLOTS), F32),
        ),
        in_specs=[pl.BlockSpec(memory_space=pltpu.HBM)] * 5,
        scratch_shapes=[
            pltpu.VMEM((32, SLOTS), F32),
            pltpu.VMEM((18, SLOTS), F32),
            pltpu.VMEM((6, SLOTS), F32),
            pltpu.VMEM((2, SLOTS), F32),
            pltpu.VMEM((1, SLOTS), jnp.int32),
            pltpu.VMEM((1, SLOTS), jnp.int32),
            pltpu.SemaphoreType.DMA((5,)),
        ],
        compiler_params=PARAMS,
        name="pack",
    )(*[pltpu.with_memory_space_constraint(x, pltpu.HBM) for x in raw])
    owned = lax.all_to_all(msg.reshape(peers, ROWS_IN, LANES), "obs", 0, 0, tiled=True)
    returned = pl.pallas_call(
        owner_kernel,
        out_shape=jax.ShapeDtypeStruct((peers * ROWS_BACK, LANES), F32),
        scratch_shapes=[
            pltpu.VMEM((RANKS * 8, LANES), jnp.int32),
            pltpu.VMEM((8 * 52, 8, LANES), F32),
            pltpu.VMEM((RANKS * 6, 8, LANES), F32),
            pltpu.VMEM((RANKS * 18, 8, LANES), F32),
            pltpu.VMEM((6, 8, LANES), F32),
            pltpu.VMEM((14, 8, LANES), jnp.int32),
        ],
        compiler_params=PARAMS,
        name="owner",
    )(owned.reshape(peers * ROWS_IN, LANES), partner)
    back = lax.all_to_all(returned.reshape(peers, 1, ROWS_BACK * LANES), "obs", 0, 0, tiled=True)
    block = jax.ShapeDtypeStruct((BLOCK, LANES), F32)
    side = jax.ShapeDtypeStruct((SIDE, 2 * SLOTS), BF16)

    def scratch(count):
        return [pltpu.VMEM((2 * count * SIDE, 2 * SLOTS), BF16), pltpu.VMEM((SIDE, LANES), F32)]

    far, right_hi, right_lo = pl.pallas_call(
        first_kernel,
        out_shape=(block, side, side),
        scratch_shapes=scratch(1) + [pltpu.VMEM((132 * 8, LANES), F32)],
        compiler_params=PARAMS,
        cost_estimate=COST,
        name="camera_0",
    )(back.reshape(peers * ROWS_BACK, LANES), own, split, pair_slot)

    def blocks(shifts):
        return pl.pallas_call(
            functools.partial(next_kernel, shifts),
                out_shape=(block,) * len(shifts),
            scratch_shapes=scratch(len(shifts)),
            compiler_params=PARAMS,
            cost_estimate=COST,
        )(own, split, right_hi, right_lo)

    def shift(x, by):
        return lax.ppermute(x, "row", [(n, (n + by) % 8) for n in range(8)])

    far = shift(far, 2)
    plus, minus = blocks((3, 5))
    plus, minus = shift(plus, 1), shift(minus, -1)
    plus2, minus2 = blocks((2, 6))
    plus1, minus1 = blocks((1, 7))
    plus2 = shift(plus2 + (plus + far), 2)
    minus2 = shift(minus2 + minus, -2)
    plus1, minus1 = shift(plus1, 1), shift(minus1, -1)
    (kept,) = blocks((0,))
    hess, grad, pair = pl.pallas_call(
        final_kernel,
        out_shape=(
            jax.ShapeDtypeStruct((CAM_ROW, 81), F32),
            jax.ShapeDtypeStruct((9, CAM_ROW), F32),
            jax.ShapeDtypeStruct((81, CAM_ROW * NBR), F32),
        ),
        scratch_shapes=[
            pltpu.VMEM((BLOCK, LANES), F32),
            pltpu.VMEM((SIDE, LANES), F32),
            pltpu.VMEM((176, LANES), F32),
        ],
        compiler_params=PARAMS,
        name="final",
    )(kept, plus1, minus1, plus2, minus2)
    return hess.T, grad, pair


def solution(mesh):
    return jax.shard_map(
        on_device,
        mesh=mesh,
        in_specs=(
            P(None, ("obs", "row")),
            P(None, ("obs", "row")),
            P(None, ("obs", "row")),
            P(("obs", "row")),
            P(("obs", "row")),
            P(("obs", "row")),
            P(None, ("obs", "row")),
            P(None, ("obs", "row")),
        ),
        out_specs=(P(None, ("obs", "row")), P(None, ("obs", "row")), P(None, ("obs", "row"))),
        check_vma=False,
    )
```
